32 devices in a mesh: rows: 4 (over y, x), cols: 8 (over z, core).
Axes of the slice: x: 2, y: 2, z: 4, core: 2. Of those that a mesh axis runs over, the one named last changes fastest.
Arguments:
- object_tiles: float32 [2, 2, 3072, 6144], P(None, None, 'rows', 'cols'), may hold values from -6 to 6
- probe: float32 [2, 512, 512], replicated, may hold values from -6 to 6
- prop_phase: float32 [512, 512], replicated, may hold values from -3.140625 to 3.140625
- amplitudes: bfloat16 [4, 8, 1, 512, 512], P('rows', 'cols'), may hold values from 0 to 2
- offsets: int32 [4, 8, 1, 2], P('rows', 'cols'), may hold values from 0 to 512
- counts: int32 [4, 8], P('rows', 'cols'), may hold values from 0 to 1
- step_size: float32 [2], replicated, may hold values from 0.3 to 1
Outputs:
- updated: float32 [2, 2, 3072, 6144], P(None, None, 'rows', 'cols')
The draws below stay inside these ranges and needn't reach their ends.
Inputs may be any that keep to these rules, and one draw needn't show every extreme that they name: `offsets`: row and column of a window's first cell in the device's tile extended by 128 cells on every side. `counts`: slots at or past a tile's count are ignored; a tile may have no probe position.
All inputs are finite; a program needn't handle non-finite values.
Results may differ from the reference program's by a relative error of at most 0.013.
The reference program's roundings to bfloat16 on the way count: a program that leaves them out, or rounds other values in their place, can miss the bound.
Values sent between devices are 32-bit elements; how exact they have to be, the bound alone decides.
A program may use at most 192 MiB of HBM per device.

```python
import math
import jax
import jax.numpy as jnp
from jax import lax

P_SIZE = 512
H = 128
TILE = 768
MAXP = 1
TROWS = 4
TCOLS = 8
NR = 3072
NC = 6144


def with_ends(entries, own_key, smallest, largest):
    extent = entries.shape
    place = [jax.random.randint(jax.random.fold_in(own_key, axis), (), 0, extent[axis]) for axis in range(len(extent))]
    entries = entries.at[tuple(place)].set(smallest)
    longest = extent.index(max(extent))
    place[longest] = (place[longest] + 1) % extent[longest]
    return entries.at[tuple(place)].set(largest)


def block_scale(stream_key, shape, cuts, least, top_value):
    loudness, own = 1.0, jax.random.fold_in(stream_key, 6)
    for dim, shards_of in cuts:
        draws = jnp.exp(jax.random.uniform(jax.random.fold_in(own, dim), (shards_of,), jnp.float32, least / len(cuts), top_value / len(cuts)))
        loudness = loudness * jnp.repeat(draws, shape[dim] // shards_of).reshape([-1 if axis == dim else 1 for axis in range(len(shape))])
    return loudness


def scatter_about(stream_key, dims, spread, reach, shards=(), kind=jnp.bfloat16):
    loudness = block_scale(stream_key, dims, shards, -0.22, 0.18) if shards else 1.0
    entries = jax.random.normal(stream_key, dims, jnp.float32) * spread * loudness
    return jnp.minimum(jnp.maximum(entries, -reach), reach).astype(kind)


def setup_inputs(seed: int = 0) -> dict:
    streams_of = jax.random.split(jax.random.key(seed), 8)
    object_tiles = scatter_about(streams_of[0], (2, 2, NR, NC), 1.0, 6.0, ((2, 4), (3, 8)), jnp.float32)
    probe = scatter_about(streams_of[1], (2, P_SIZE, P_SIZE), 1.0, 6.0, (), jnp.float32)
    prop_phase = jnp.clip(jax.random.uniform(streams_of[2], (P_SIZE, P_SIZE), jnp.float32, -3.140625, 3.140625), -3.140625, 3.140625)
    amplitudes = jnp.clip(2.0 * jax.random.uniform(streams_of[3], (TROWS, TCOLS, MAXP, P_SIZE, P_SIZE), jnp.float32) ** block_scale(streams_of[3], (TROWS, TCOLS, MAXP, P_SIZE, P_SIZE), ((0, 4), (1, 8)), -0.2, 0.2), 0.0, 2.0).astype(jnp.bfloat16)
    offsets = with_ends(jax.random.randint(streams_of[4], (TROWS, TCOLS, MAXP, 2), 0, TILE + 2 * H - P_SIZE + 1), jax.random.fold_in(streams_of[4], 1), 0, TILE + 2 * H - P_SIZE).astype(jnp.int32)
    counts = with_ends(jax.random.randint(streams_of[5], (TROWS, TCOLS), 0, MAXP + 1), jax.random.fold_in(streams_of[5], 1), 0, MAXP).astype(jnp.int32)
    step_size = jnp.clip(jnp.exp(jax.random.uniform(streams_of[6], (2,), jnp.float32, math.log(0.3), math.log(1.0))), 0.3, 1.0)
    return {"object_tiles": object_tiles, "probe": probe, "prop_phase": prop_phase, "amplitudes": amplitudes, "offsets": offsets, "counts": counts, "step_size": step_size}


def dft_tables(length, inverse):
    index = jnp.arange(length, dtype=jnp.int32)
    product = index[:, None] * index[None, :] % length
    angles = product.astype(jnp.float32) * (2.0 * math.pi / length)
    scaling = 1.0 / math.sqrt(length)
    direction = 1.0 if inverse else -1.0
    return ((jnp.cos(angles) * scaling).astype(jnp.bfloat16), (direction * jnp.sin(angles) * scaling).astype(jnp.bfloat16))

def transform(real_part, imag_part, tables):
    table_re, table_im = tables
    left_re = real_part.astype(jnp.bfloat16)
    left_im = imag_part.astype(jnp.bfloat16)
    mid_re = jnp.dot(table_re, left_re, preferred_element_type=jnp.float32) - jnp.dot(table_im, left_im, preferred_element_type=jnp.float32)
    mid_im = jnp.dot(table_re, left_im, preferred_element_type=jnp.float32) + jnp.dot(table_im, left_re, preferred_element_type=jnp.float32)
    mid_re = mid_re.astype(jnp.bfloat16)
    mid_im = mid_im.astype(jnp.bfloat16)
    out_re = jnp.dot(mid_re, table_re, preferred_element_type=jnp.float32) - jnp.dot(mid_im, table_im, preferred_element_type=jnp.float32)
    out_im = jnp.dot(mid_re, table_im, preferred_element_type=jnp.float32) + jnp.dot(mid_im, table_re, preferred_element_type=jnp.float32)
    return (out_re, out_im)

def probe_gradient(window, probe, kernel_re, kernel_im, measured, forward, backward):
    first_re, first_im = (window[0, 0], window[0, 1])
    second_re, second_im = (window[1, 0], window[1, 1])
    probe_re, probe_im = (probe[0], probe[1])
    wave_re = probe_re * first_re - probe_im * first_im
    wave_im = probe_re * first_im + probe_im * first_re
    spec_re, spec_im = transform(wave_re, wave_im, forward)
    prop_re = spec_re * kernel_re - spec_im * kernel_im
    prop_im = spec_re * kernel_im + spec_im * kernel_re
    psi1_re, psi1_im = transform(prop_re, prop_im, backward)
    exit_re = psi1_re * second_re - psi1_im * second_im
    exit_im = psi1_re * second_im + psi1_im * second_re
    far_re, far_im = transform(exit_re, exit_im, forward)
    magnitude = jnp.sqrt(far_re * far_re + far_im * far_im + 1.0)
    factor = 1.0 - measured.astype(jnp.float32) / magnitude
    chi2_re, chi2_im = transform(far_re * factor, far_im * factor, backward)
    grad2_re = psi1_re * chi2_re + psi1_im * chi2_im
    grad2_im = psi1_re * chi2_im - psi1_im * chi2_re
    back_re = second_re * chi2_re + second_im * chi2_im
    back_im = second_re * chi2_im - second_im * chi2_re
    bspec_re, bspec_im = transform(back_re, back_im, forward)
    bprop_re = bspec_re * kernel_re + bspec_im * kernel_im
    bprop_im = bspec_im * kernel_re - bspec_re * kernel_im
    dwave_re, dwave_im = transform(bprop_re, bprop_im, backward)
    grad1_re = probe_re * dwave_re + probe_im * dwave_im
    grad1_im = probe_re * dwave_im - probe_im * dwave_re
    return jnp.stack([jnp.stack([grad1_re, grad1_im]), jnp.stack([grad2_re, grad2_im])])

def reference(object_tiles, probe, prop_phase, amplitudes, offsets, counts, step_size):
    padded = jnp.pad(object_tiles, ((0, 0), (0, 0), (H, H), (H, H)))
    forward = dft_tables(P_SIZE, False)
    backward = dft_tables(P_SIZE, True)
    kernel_re = jnp.cos(prop_phase)
    kernel_im = jnp.sin(prop_phase)
    zero = jnp.int32(0)
    total = TROWS * TCOLS * MAXP

    def visit(grad, index):
        tile_row = (index // (TCOLS * MAXP)).astype(jnp.int32)
        tile_col = (index // MAXP % TCOLS).astype(jnp.int32)
        slot = (index % MAXP).astype(jnp.int32)
        start_row = (tile_row * TILE + offsets[tile_row, tile_col, slot, 0]).astype(jnp.int32)
        start_col = (tile_col * TILE + offsets[tile_row, tile_col, slot, 1]).astype(jnp.int32)
        corner = (zero, zero, start_row, start_col)

        def compute(unused):
            window = lax.dynamic_slice(padded, corner, (2, 2, P_SIZE, P_SIZE))
            return probe_gradient(window, probe, kernel_re, kernel_im, amplitudes[tile_row, tile_col, slot], forward, backward)

        def nothing(unused):
            return jnp.zeros((2, 2, P_SIZE, P_SIZE), jnp.float32)
        contribution = lax.cond(slot < counts[tile_row, tile_col], compute, nothing, 0)
        current = lax.dynamic_slice(grad, corner, (2, 2, P_SIZE, P_SIZE))
        return (lax.dynamic_update_slice(grad, current + contribution, corner), None)
    grad, unused = lax.scan(visit, jnp.zeros(padded.shape, jnp.float32), jnp.arange(total, dtype=jnp.int32))
    grad = grad[:, :, H:H + NR, H:H + NC]
    return object_tiles - step_size[:, None, None, None] * grad
```

```python
import functools
import math

import jax
import jax.numpy as jnp
import numpy as np
from jax import lax
from jax.experimental import pallas as pl
from jax.experimental.pallas import tpu as pltpu
from jax.sharding import PartitionSpec as P

H = 128
LANES = 128
SUBLANES = 8
ROWS = 512
F32 = jnp.float32
BF16 = jnp.bfloat16
MESH = pl.DeviceIdType.MESH


def dft_table(length):
    index = np.arange(length, dtype=np.int64)
    angles = ((index[:, None] * index[None, :]) % length).astype(np.float32) * np.float32(
        2.0 * math.pi / length
    )
    scaling = np.float32(1.0 / math.sqrt(length))
    return (
        jnp.asarray((np.cos(angles) * scaling).astype(BF16)),
        jnp.asarray((-np.sin(angles) * scaling).astype(BF16)),
    )


def make_tables(cos_ref, sin_ref, fwd, bwd):
    n = cos_ref.shape[0]
    c, s = cos_ref[...], sin_ref[...]
    for table, sine in ((fwd, s), (bwd, -s)):
        table[:n, :n] = c
        table[n:, n:] = c
        table[n:, :n] = sine
        table[:n, n:] = -sine


def transform(src, left, right, mid, epilogue):
    n = mid.shape[0]

    @pl.loop(0, n // ROWS)
    def _(i):
        at = pl.ds(pl.multiple_of(i * ROWS, ROWS), ROWS)
        low = pl.ds(pl.multiple_of(n + i * ROWS, ROWS), ROWS)
        mid[at, :n] = jnp.dot(left[at, :], src[...], preferred_element_type=F32).astype(BF16)
        mid[at, n:] = jnp.dot(left[low, :], src[...], preferred_element_type=F32).astype(BF16)

    @pl.loop(0, n // ROWS)
    def _(i):
        at = pl.ds(pl.multiple_of(i * ROWS, ROWS), ROWS)
        low = pl.ds(pl.multiple_of(n + i * ROWS, ROWS), ROWS)
        out = jnp.dot(mid[at, :], right[...], preferred_element_type=F32)
        epilogue(i, at, low, out[:, :n], out[:, n:])


class Copies:
    def __init__(self, sends, receives, locals_):
        self.sends, self.receives, self.locals = sends, receives, locals_
        self.remote_used = self.local_used = 0

    def remote(self, src, dst, there, here, device):
        k = self.remote_used
        self.remote_used += 1
        copy = pltpu.make_async_remote_copy(
            src_ref=src,
            dst_ref=dst,
            send_sem=self.sends.at[k],
            recv_sem=self.receives.at[k],
            device_id=device,
            device_id_type=MESH,
        )
        return Remote(copy, there, here)

    def local(self, src, dst):
        k = self.local_used
        self.local_used += 1
        return pltpu.make_async_copy(src, dst, self.locals.at[k])


class Remote:
    def __init__(self, copy, there, here):
        self.copy, self.there, self.here = copy, there, here

    def start(self):
        pl.when(self.there)(lambda: self.copy.start())

    def arrived(self):
        pl.when(self.here)(lambda: self.copy.wait_recv())

    def sent(self):
        pl.when(self.there)(lambda: self.copy.wait_send())


REMOTES = 2 + 2 * 18
LOCALS = 5 + 2 * 3 + 2 * 3


def step_kernel(
    offs_ref, count_ref, step_ref, meta, obj, probe_in, phase_in, amp_in, cos_in, sin_in, out,
    near, probe, k, amp, cos, sin, fwd, bwd, src, mid, psi,
    et0, et1, eb0, eb1, m0, m1, body0, body1, xs, xr, ss, sr, gz0, gz1,
    orr, ox, own_l, own_r, got_l, got_r, near_l, near_r,
    sends, receives, locals_,
):
    n = cos.shape[0]
    tile_rows, inner = obj.shape[2:]
    wide = inner + 2 * H
    tall = tile_rows + 2 * H
    half = (tall - n) // 2
    last = tile_rows - H
    ets, ebs, ms, bodies, gzs = (et0, et1), (eb0, eb1), (m0, m1), (body0, body1), (gz0, gz1)

    me_r, me_c = lax.axis_index("rows"), lax.axis_index("cols")
    n_r, n_c = lax.axis_size("rows"), lax.axis_size("cols")
    even = lax.rem(me_r, 2) == 0
    side = jnp.where(even, 1, -1)
    has_left, has_right = me_c > 0, me_c < n_c - 1
    has_above, has_below = me_r > 0, me_r < n_r - 1
    far_above, far_below = me_r > 1, me_r < n_r - 2
    row = lambda r: {"rows": r, "cols": me_c}
    col = lambda c: {"rows": me_r, "cols": c}
    partner = row(me_r + side)
    outward = row(me_r - 2 * side)
    inward = row(me_r + 2 * side)
    has_outward = jnp.where(even, me_r - 2, n_r - 3 - me_r) >= 0
    has_inward = jnp.where(even, n_r - 3 - me_r, me_r - 2) >= 0
    always = me_r >= 0

    copies = Copies(sends, receives, locals_)
    load_small = [
        copies.local(a, b)
        for a, b in ((cos_in, cos), (sin_in, sin), (probe_in, probe), (phase_in, k.at[0]), (amp_in.at[0, 0, 0], amp))
    ]
    load_edges, load_body = [], []
    centre = pl.ds(H, inner)
    for s in range(2):
        load_edges.append(
            [
                copies.local(obj.at[s, :, 0:H, :], ets[s].at[:, :, centre]),
                copies.local(obj.at[s, :, last : last + H, :], ebs[s].at[:, :, centre]),
            ]
        )
        load_body.append(copies.local(obj.at[s, :, H:last, :], ms[s].at[:, :, centre]))
    for c in load_edges[0] + load_edges[1]:
        c.start()
    for c in load_small[:2]:
        c.start()
    for c in load_body:
        c.start()
    for c in load_small[2:]:
        c.start()

    barrier = pltpu.get_barrier_semaphore()
    greeted = (
        (has_left, col(me_c - 1)), (has_right, col(me_c + 1)),
        (has_above, row(me_r - 1)), (has_below, row(me_r + 1)),
        (far_above, row(me_r - 2)), (far_below, row(me_r + 2)),
    )
    total = jnp.int32(0)
    for exists, device in greeted:
        total += exists.astype(jnp.int32)

        @pl.when(exists)
        def _(device=device):
            pl.semaphore_signal(barrier, inc=1, device_id=device, device_id_type=MESH)

    @pl.when(jnp.logical_not(has_left))
    def _():
        for ref in ets + ebs + ms:
            ref[:, :, :H] = jnp.zeros((2, ref.shape[1], H), F32)
        got_l[...] = jnp.zeros_like(got_l)
        near_l[...] = jnp.zeros_like(near_l)

    @pl.when(jnp.logical_not(has_right))
    def _():
        for ref in ets + ebs + ms:
            ref[:, :, H + inner :] = jnp.zeros((2, ref.shape[1], H), F32)
        got_r[...] = jnp.zeros_like(got_r)
        near_r[...] = jnp.zeros_like(near_r)

    @pl.when(jnp.logical_not(has_inward))
    def _():
        xr[...] = jnp.zeros_like(xr)

    @pl.when(jnp.logical_not(has_outward))
    def _():
        ox[...] = jnp.zeros_like(ox)

    @pl.when(jnp.logical_not(has_above))
    def _():
        near[0] = jnp.zeros(near.shape[1:], jnp.int32)

    @pl.when(jnp.logical_not(has_below))
    def _():
        near[1] = jnp.zeros(near.shape[1:], jnp.int32)

    pl.semaphore_wait(barrier, total)

    metas = [
        copies.remote(meta, near.at[0], has_below, has_above, row(me_r + 1)),
        copies.remote(meta, near.at[1], has_above, has_below, row(me_r - 1)),
    ]
    to_right = lambda a, b: copies.remote(a, b, has_right, has_left, col(me_c + 1))
    to_left = lambda a, b: copies.remote(a, b, has_left, has_right, col(me_c - 1))
    halo_edges, halo_body = [], []
    for s in range(2):
        both = []
        for ref, lo in ((ets[s], 0), (ebs[s], last)):
            both.append(to_right(obj.at[s, :, lo : lo + H, inner - H :], ref.at[:, :, 0:H]))
            both.append(to_left(obj.at[s, :, lo : lo + H, 0:H], ref.at[:, :, H + inner :]))
        halo_edges.append(both)
        halo_body.append(
            [
                to_right(obj.at[s, :, H:last, inner - H :], ms[s].at[:, :, 0:H]),
                to_left(obj.at[s, :, H:last, 0:H], ms[s].at[:, :, H + inner :]),
            ]
        )
    for c in metas + halo_edges[0] + halo_edges[1] + halo_body[0] + halo_body[1]:
        c.start()

    my_row, my_col = offs_ref[0], offs_ref[1]
    weight = jnp.where(count_ref[0] > 0, 1.0, 0.0).astype(F32)
    for c in metas:
        c.arrived()
    above_row, above_col = jnp.max(near[0, 0]), jnp.max(near[0, 1])
    below_row, below_col = jnp.max(near[1, 0]), jnp.max(near[1, 1])
    mate_row = jnp.where(even, below_row, above_row)
    mate_col = jnp.where(even, below_col, above_col)
    far_col = jnp.where(even, above_col, below_col)

    def take_columns(ref, part, at, start):
        return pltpu.roll(ref[part, at, :], lax.rem(wide - start, wide), axis=1)[:, :n]

    def take_rows(field, part, start, offset, height):
        strips = [field[part, q, pl.ds(start + offset, height), :] for q in range(n // LANES)]
        return jnp.concatenate(strips, axis=1)

    def put_rows(field, part, rows, value):
        for q in range(n // LANES):
            field[part, q, rows, :] = value[:, q * LANES : (q + 1) * LANES]

    every = pl.ds(0, H)

    outers, inners = [], []
    for s in range(2):
        outers.append([copies.remote(xs.at[s, p], xr.at[s, p], has_outward, has_inward, outward) for p in range(2)])
        inners.append([copies.remote(ss.at[s, p], sr.at[s, p], always, always, partner) for p in range(2)])
    for s in range(2):
        for c in load_edges[s]:
            c.wait()
        for c in halo_edges[s]:
            c.arrived()
        for p in range(2):
            top = take_columns(ets[s], p, every, far_col)
            bottom = take_columns(ebs[s], p, every, far_col)
            xs[s, p] = jnp.where(even, top, bottom)
            outers[s][p].start()
            top = take_columns(ets[s], p, every, mate_col)
            bottom = take_columns(ebs[s], p, every, mate_col)
            ss[s, p] = jnp.where(even, bottom, top)

    mate_near = jnp.where(even, mate_row <= half, mate_row > half)

    def pass_on(s, p):
        outers[s][p].arrived()
        ss[s, p] = jnp.where(mate_near, ss[s, p], xr[s, p])
        inners[s][p].start()

    for c in load_small:
        c.wait()
    make_tables(cos, sin, fwd, bwd)
    for gz in gzs:
        for lo, hi in ((0, tall - n - H), (tall - H, gz.shape[2])):

            @pl.loop(0, n // LANES)
            def _(q, gz=gz, lo=lo, hi=hi):
                for p in range(2):
                    gz[p, q, lo:hi, :] = jnp.zeros((hi - lo, LANES), F32)

    def fill_body(s):
        load_body[s].wait()
        for c in halo_body[s]:
            c.arrived()
        for p in range(2):
            put_rows(bodies[s], p, slice(H, 2 * H), take_columns(ets[s], p, every, my_col))
            put_rows(bodies[s], p, slice(H + last, 2 * H + last), take_columns(ebs[s], p, every, my_col))

            @pl.loop(0, (last - H) // H)
            def _(i, p=p):
                at = pl.ds(pl.multiple_of(i * H, H), H)
                to = pl.ds(pl.multiple_of(2 * H + i * H, H), H)
                put_rows(bodies[s], p, to, take_columns(ms[s], p, at, my_col))

    fill_body(0)

    @pl.loop(0, n // H)
    def _(i):
        at = pl.ds(pl.multiple_of(i * H, H), H)
        phase = k[0, at, :]
        k[1, at, :] = jnp.sin(phase)
        k[0, at, :] = jnp.cos(phase)

    pass_on(0, 0)
    pass_on(0, 1)
    fill_body(1)

    def halo_rows(s):
        for p in range(2):
            inners[s][p].arrived()
            block = sr[s, p]
            put_rows(bodies[s], p, slice(0, H), block)
            put_rows(bodies[s], p, slice(tall - H, tall), block)

    window = lambda s, p, offset, height: take_rows(bodies[s], p, my_row, offset, height)

    halo_rows(0)
    pass_on(1, 0)

    @pl.loop(0, n // H)
    def _(i):
        at = pl.ds(pl.multiple_of(i * H, H), H)
        low = pl.ds(pl.multiple_of(n + i * H, H), H)
        a_re = window(0, 0, i * H, H)
        a_im = window(0, 1, i * H, H)
        q_re, q_im = probe[0, at, :], probe[1, at, :]
        src[at, :] = (q_re * a_re - q_im * a_im).astype(BF16)
        src[low, :] = (q_re * a_im + q_im * a_re).astype(BF16)

    def propagate(i, at, low, re, im):
        k_re, k_im = k[0, at, :], k[1, at, :]
        src[at, :] = (re * k_re - im * k_im).astype(BF16)
        src[low, :] = (re * k_im + im * k_re).astype(BF16)

    def keep(i, at, low, re, im):
        psi[0, at, :] = re
        psi[1, at, :] = im

    transform(src, fwd, bwd, mid, propagate)
    pass_on(1, 1)
    transform(src, bwd, fwd, mid, keep)

    halo_rows(1)

    @pl.loop(0, n // H)
    def _(i):
        at = pl.ds(pl.multiple_of(i * H, H), H)
        low = pl.ds(pl.multiple_of(n + i * H, H), H)
        b_re = window(1, 0, i * H, H)
        b_im = window(1, 1, i * H, H)
        p_re, p_im = psi[0, at, :], psi[1, at, :]
        src[at, :] = (p_re * b_re - p_im * b_im).astype(BF16)
        src[low, :] = (p_re * b_im + p_im * b_re).astype(BF16)

    def detect(i, at, low, re, im):
        factor = 1.0 - amp[at, :].astype(F32) / jnp.sqrt(re * re + im * im + 1.0)
        src[at, :] = (re * factor).astype(BF16)
        src[low, :] = (im * factor).astype(BF16)

    first_row = tall - n - H

    def spread(i, at, low, re, im):
        p_re, p_im = psi[0, at, :], psi[1, at, :]
        b_re = window(1, 0, i * ROWS, ROWS)
        b_im = window(1, 1, i * ROWS, ROWS)
        to = pl.ds(pl.multiple_of(first_row + i * ROWS, SUBLANES), ROWS)
        put_rows(gz1, 0, to, weight * (p_re * re + p_im * im))
        put_rows(gz1, 1, to, weight * (p_re * im - p_im * re))
        src[at, :] = (b_re * re + b_im * im).astype(BF16)
        src[low, :] = (b_re * im - b_im * re).astype(BF16)

    transform(src, fwd, bwd, mid, detect)
    transform(src, bwd, fwd, mid, spread)

    spills, relays = [], []
    for s in range(2):
        spills.append([copies.remote(ss.at[s, p], orr.at[s, p], always, always, partner) for p in range(2)])
        relays.append([copies.remote(orr.at[s, p], ox.at[s, p], has_inward, has_outward, inward) for p in range(2)])

    def spill(s):
        start = jnp.where(my_row <= half, first_row - my_row, first_row + tile_rows + H - my_row)
        for p in range(2):
            inners[s][p].sent()
            ss[s, p] = take_rows(gzs[s], p, start, 0, H)
            spills[s][p].start()

    def relay(s, p):
        spills[s][p].arrived()
        relays[s][p].start()

    def back(i, at, low, re, im):
        k_re, k_im = k[0, at, :], k[1, at, :]
        src[at, :] = (re * k_re + im * k_im).astype(BF16)
        src[low, :] = (im * k_re - re * k_im).astype(BF16)

    def finish(i, at, low, re, im):
        q_re, q_im = probe[0, at, :], probe[1, at, :]
        to = pl.ds(pl.multiple_of(first_row + i * ROWS, SUBLANES), ROWS)
        put_rows(gz0, 0, to, weight * (q_re * re + q_im * im))
        put_rows(gz0, 1, to, weight * (q_re * im - q_im * re))

    spill(1)
    transform(src, fwd, bwd, mid, back)
    relay(1, 0)
    transform(src, bwd, fwd, mid, finish)
    spill(0)
    relay(1, 1)

    spread_out = lambda block, start: pltpu.roll(
        jnp.concatenate([block, jnp.zeros((block.shape[0], wide - n), F32)], axis=1), start, axis=1
    )

    def place_rows(s, p, ref, offset, at):
        block = spread_out(take_rows(gzs[s], p, tall - n - my_row, offset, H), my_col)
        rows = pl.ds(pl.multiple_of(offset, H), H)
        own_l[s, p, rows, :] = block[:, :H]
        own_r[s, p, rows, :] = block[:, H + inner :]
        ref[p, at, H : H + inner] -= step_ref[s] * block[:, H : H + inner]

    early, lates = [], []
    for s in range(2):
        early.append([to_left(own_l.at[s], got_r.at[s]), to_right(own_r.at[s], got_l.at[s])])
        lates.append([to_left(xs.at[s, :, :, : 2 * H], near_r.at[s]), to_right(xs.at[s, :, :, 2 * H : 4 * H], near_l.at[s])])

    def place_own(s):
        for p in range(2):
            place_rows(s, p, ets[s], 0, every)
            place_rows(s, p, ebs[s], last, every)

            @pl.loop(0, (last - H) // H)
            def _(i, p=p):
                place_rows(s, p, ms[s], H + i * H, pl.ds(pl.multiple_of(i * H, H), H))

        for c in early[s]:
            c.start()

    def place_near(s):
        for p in range(2):
            relays[s][p].arrived()
            outers[s][p].sent()
        for p in range(2):
            for ref, e, mine, start in (
                (ets[s], 0, jnp.logical_and(has_above, above_row > half), above_col),
                (ebs[s], 1, jnp.logical_and(has_below, below_row <= half), below_col),
            ):
                outer = even if e == 0 else jnp.logical_not(even)
                block = jnp.where(outer, ox[s, p], orr[s, p])
                block = spread_out(jnp.where(mine, block, jnp.zeros_like(block)), start)
                xs[s, p, :, e * H : (e + 1) * H] = block[:, :H]
                xs[s, p, :, (2 + e) * H : (3 + e) * H] = block[:, H + inner :]
                ref[p, :, H : H + inner] -= step_ref[s] * block[:, H : H + inner]
        for c in lates[s]:
            c.start()

    outs = []
    for s in range(2):
        outs.append(
            [
                copies.local(ms[s].at[:, :, centre], out.at[s, :, H:last, :]),
                copies.local(ets[s].at[:, :, centre], out.at[s, :, 0:H, :]),
                copies.local(ebs[s].at[:, :, centre], out.at[s, :, last : last + H, :]),
            ]
        )

    def sides_body(s):
        for c in early[s]:
            c.arrived()
        for p in range(2):

            @pl.loop(0, (last - H) // H)
            def _(i, p=p):
                at = pl.ds(pl.multiple_of(i * H, H), H)
                rows = pl.ds(pl.multiple_of(H + i * H, H), H)
                ms[s][p, at, H : 2 * H] -= step_ref[s] * got_l[s, p, rows, :]
                ms[s][p, at, inner : H + inner] -= step_ref[s] * got_r[s, p, rows, :]

        outs[s][0].start()

    def sides_edges(s):
        for c in lates[s]:
            c.arrived()
        for p in range(2):
            for ref, e, lo in ((ets[s], 0, 0), (ebs[s], 1, last)):
                ref[p, :, H : 2 * H] -= step_ref[s] * (got_l[s, p, lo : lo + H, :] + near_l[s, p, :, e * H : (e + 1) * H])
                ref[p, :, inner : H + inner] -= step_ref[s] * (got_r[s, p, lo : lo + H, :] + near_r[s, p, :, e * H : (e + 1) * H])
        for c in outs[s][1:]:
            c.start()

    place_own(1)
    relay(0, 0)
    place_own(0)
    relay(0, 1)
    place_near(1)
    sides_body(1)
    sides_body(0)
    sides_edges(1)
    place_near(0)
    sides_edges(0)

    for group in [metas] + halo_edges + halo_body + spills + relays + early + lates:
        for c in group:
            c.sent()
    for group in outs:
        for c in group:
            c.wait()
    assert copies.remote_used == REMOTES and copies.local_used == LOCALS


def per_device(object_tiles, probe, prop_phase, amplitudes, offsets, counts, step_size):
    n = probe.shape[1]
    rows, inner = object_tiles.shape[2:]
    cos, sin = dft_table(n)
    mine = offsets[0, 0, 0]
    meta = jnp.broadcast_to(mine[:, None, None], (2, SUBLANES, LANES))
    tall, wide = rows + 2 * H, inner + 2 * H
    smem = pl.BlockSpec(memory_space=pltpu.SMEM)
    anywhere = pl.BlockSpec(memory_space=pl.ANY)
    vmem = lambda *shape, kind=F32: pltpu.VMEM(shape, kind)
    edge, body = vmem(2, H, wide), vmem(2, rows - 2 * H, wide)
    strip, late = vmem(2, 2, rows, H), vmem(2, 2, H, 2 * H)
    block = vmem(2, 2, H, n)
    gz = vmem(2, n // LANES, 2 * tall - n - 2 * H, LANES)
    scratch = (
        [vmem(2, 2, SUBLANES, LANES, kind=jnp.int32), vmem(2, n, n), vmem(2, n, n), vmem(n, n, kind=BF16)]
        + [vmem(n, n, kind=BF16)] * 2
        + [vmem(2 * n, 2 * n, kind=BF16)] * 2
        + [vmem(2 * n, n, kind=BF16), vmem(n, 2 * n, kind=BF16), vmem(2, n, n)]
        + [edge] * 4
        + [body] * 2
        + [vmem(2, n // LANES, tall, LANES)] * 2
        + [block] * 4
        + [gz] * 2
        + [block] * 2
        + [strip] * 4
        + [late] * 2
        + [pltpu.SemaphoreType.DMA((REMOTES,))] * 2
        + [pltpu.SemaphoreType.DMA((LOCALS,))]
    )
    return pl.pallas_call(
        step_kernel,
        in_specs=[smem] * 3 + [anywhere] * 7,
        out_specs=anywhere,
        out_shape=jax.ShapeDtypeStruct(object_tiles.shape, F32),
        scratch_shapes=scratch,
        name="step",
        compiler_params=pltpu.CompilerParams(
            collective_id=0, has_side_effects=True, vmem_limit_bytes=67043328
        ),
    )(mine, counts[0], step_size, meta, object_tiles, probe, prop_phase, amplitudes, cos, sin)


def solution(mesh):
    return jax.shard_map(
        per_device,
        mesh=mesh,
        in_specs=(
            P(None, None, "rows", "cols"),
            P(),
            P(),
            P("rows", "cols", None, None, None),
            P("rows", "cols", None, None),
            P("rows", "cols"),
            P(),
        ),
        out_specs=P(None, None, "rows", "cols"),
        check_vma=False,
    )
```

```python
import math

import jax
import jax.numpy as jnp
import numpy as np
from jax import lax
from jax.experimental import pallas as pl
from jax.experimental.pallas import tpu as pltpu
from jax.sharding import PartitionSpec as P

H = 128
LANES = 128
SUBLANES = 8
PARTS = 2
F32 = jnp.float32
BF16 = jnp.bfloat16
MESH = pl.DeviceIdType.MESH


def dft_table(length):
    index = np.arange(length, dtype=np.int64)
    angles = ((index[:, None] * index[None, :]) % length).astype(np.float32) * np.float32(
        2.0 * math.pi / length
    )
    scaling = np.float32(1.0 / math.sqrt(length))
    return (
        jnp.asarray((np.cos(angles) * scaling).astype(BF16)),
        jnp.asarray((-np.sin(angles) * scaling).astype(BF16)),
    )


def make_tables(cos_ref, sin_ref, fwd, bwd):
    n = cos_ref.shape[0]
    c, s = cos_ref[...], sin_ref[...]
    for table, sine in ((fwd, s), (bwd, -s)):
        table[:n, :n] = c
        table[n:, n:] = c
        table[n:, :n] = sine
        table[:n, n:] = -sine


class Copies:
    def __init__(self, sends, receives, locals_):
        self.sends, self.receives, self.locals = sends, receives, locals_
        self.remotes = []
        self.local_used = 0

    def remote(self, src, dst, there, here, device):
        k = len(self.remotes)
        copy = pltpu.make_async_remote_copy(
            src_ref=src,
            dst_ref=dst,
            send_sem=self.sends.at[k],
            recv_sem=self.receives.at[k],
            device_id=device,
            device_id_type=MESH,
        )
        self.remotes.append(Remote(copy, there, here))
        return self.remotes[-1]

    def local(self, src, dst):
        k = self.local_used
        self.local_used += 1
        return pltpu.make_async_copy(src, dst, self.locals.at[k])


class Remote:
    def __init__(self, copy, there, here):
        self.copy, self.there, self.here = copy, there, here
        self.waited = False

    def start(self):
        pl.when(self.there)(lambda: self.copy.start())

    def arrived(self):
        pl.when(self.here)(lambda: self.copy.wait_recv())

    def sent(self):
        self.waited = True
        pl.when(self.there)(lambda: self.copy.wait_send())


REMOTES = 4 + 2 * (8 + 12 * PARTS)
LOCALS = 5 + 2 * 3


def step_kernel(
    offs_ref, count_ref, step_ref, obj, probe_in, phase_in, amp_in, cos_in, sin_in, out,
    meta, near, probe, k, amp, cos, sin, fwd, bwd, src, mid, psi,
    hl, hr, body0, body1, xs, xr, ss, sr, gz0, gz1,
    orr, ox, own_l, own_r, gl0, gl1, gr0, gr1, near_l, near_r,
    sends, receives, locals_,
):
    n = cos.shape[0]
    tile_rows, inner = obj.shape[2:]
    wide = inner + 2 * H
    tall = tile_rows + 2 * H
    half = (tall - n) // 2
    last = tile_rows - H
    bodies, gzs, gls, grs = (body0, body1), (gz0, gz1), (gl0, gl1), (gr0, gr1)

    me_r, me_c = lax.axis_index("rows"), lax.axis_index("cols")
    n_r, n_c = lax.axis_size("rows"), lax.axis_size("cols")
    odd = lax.rem(me_r, 2)
    even = odd == 0
    side = 1 - 2 * odd
    has_left, has_right = me_c > 0, me_c < n_c - 1
    has_above, has_below = me_r > 0, me_r < n_r - 1
    far_above, far_below = me_r > 1, me_r < n_r - 2
    row = lambda r: {"rows": r, "cols": me_c}
    col = lambda c: {"rows": me_r, "cols": c}
    partner = row(me_r + side)
    outward = row(me_r - 2 * side)
    inward = row(me_r + 2 * side)
    has_outward = jnp.where(even, me_r - 2, n_r - 3 - me_r) >= 0
    has_inward = jnp.where(even, n_r - 3 - me_r, me_r - 2) >= 0
    always = me_r >= 0

    copies = Copies(sends, receives, locals_)
    far_rows = pl.ds(pl.multiple_of(odd * last, H), H)
    mate_rows = pl.ds(pl.multiple_of((1 - odd) * last, H), H)
    mid_rows = pl.ds(H, last - H)
    pieces = (far_rows, mate_rows, mid_rows)

    loads = [[copies.local(obj.at[s, :, at, :], out.at[s, :, at, :]) for at in pieces] for s in range(2)]
    load_small = [
        copies.local(a, b)
        for a, b in ((cos_in, cos), (sin_in, sin), (phase_in, k.at[0]), (probe_in, probe), (amp_in.at[0, 0, 0], amp))
    ]
    for c in loads[0][:2] + loads[1][:2] + load_small[:3] + loads[0][2:] + load_small[3:] + loads[1][2:]:
        c.start()
    for i in range(2):
        meta[i] = jnp.full(meta.shape[1:], offs_ref[i], jnp.int32)

    barrier = pltpu.get_barrier_semaphore()
    greeted = (
        (has_left, col(me_c - 1)), (has_right, col(me_c + 1)),
        (has_above, row(me_r - 1)), (has_below, row(me_r + 1)),
        (far_above, row(me_r - 2)), (far_below, row(me_r + 2)),
    )
    total = jnp.int32(0)
    for exists, device in greeted:
        total += exists.astype(jnp.int32)

        @pl.when(exists)
        def _(device=device):
            pl.semaphore_signal(barrier, inc=1, device_id=device, device_id_type=MESH)

    first_row = tall - n - H

    @pl.when(jnp.logical_not(has_left))
    def _():
        hl[...] = jnp.zeros_like(hl)
        near_l[...] = jnp.zeros_like(near_l)
        for ref in gls:
            ref[:, first_row : first_row + n, :] = jnp.zeros((2, n, H), F32)

    @pl.when(jnp.logical_not(has_right))
    def _():
        hr[...] = jnp.zeros_like(hr)
        near_r[...] = jnp.zeros_like(near_r)
        for ref in grs:
            ref[:, first_row : first_row + n, :] = jnp.zeros((2, n, H), F32)

    @pl.when(jnp.logical_not(has_inward))
    def _():
        xr[...] = jnp.zeros_like(xr)

    @pl.when(jnp.logical_not(has_outward))
    def _():
        ox[...] = jnp.zeros_like(ox)

    for i, exists in enumerate((has_above, has_below, has_left, has_right)):

        @pl.when(jnp.logical_not(exists))
        def _(i=i):
            near[i] = jnp.zeros(near.shape[1:], jnp.int32)

    pl.semaphore_wait(barrier, total)

    to_right = lambda a, b: copies.remote(a, b, has_right, has_left, col(me_c + 1))
    to_left = lambda a, b: copies.remote(a, b, has_left, has_right, col(me_c - 1))
    metas = [
        copies.remote(meta, near.at[0], has_below, has_above, row(me_r + 1)),
        copies.remote(meta, near.at[1], has_above, has_below, row(me_r - 1)),
        to_right(meta, near.at[2]),
        to_left(meta, near.at[3]),
    ]
    halos = [
        [
            [
                to_right(obj.at[s, :, at, inner - H :], hl.at[s, :, at, :]),
                to_left(obj.at[s, :, at, 0:H], hr.at[s, :, at, :]),
            ]
            for at in pieces
        ]
        for s in range(2)
    ]
    for group in (metas, halos[0][0], halos[0][1], halos[1][0], halos[1][1], halos[0][2], halos[1][2]):
        for c in group:
            c.start()

    for lo, hi in ((0, first_row), (first_row + n, gz0.shape[2])):

        @pl.loop(0, n // LANES)
        def _(q, lo=lo, hi=hi):
            for gz in gzs:
                for p in range(2):
                    gz[p, q, lo:hi, :] = jnp.zeros((hi - lo, LANES), F32)

        for ref in gls + grs:
            ref[:, lo:hi, :] = jnp.zeros((2, hi - lo, H), F32)

    my_row, my_col = offs_ref[0], offs_ref[1]
    weight = jnp.where(count_ref[0] > 0, 1.0, 0.0).astype(F32)
    for c in metas:
        c.arrived()
    above_row, above_col = jnp.max(near[0, 0]), jnp.max(near[0, 1])
    below_row, below_col = jnp.max(near[1, 0]), jnp.max(near[1, 1])
    left_row, right_row = jnp.max(near[2, 0]), jnp.max(near[3, 0])
    mate_row = jnp.where(even, below_row, above_row)
    mate_col = jnp.where(even, below_col, above_col)
    far_col = jnp.where(even, above_col, below_col)

    def take_columns(s, p, at, start):
        line = jnp.concatenate([hl[s, p, at, :], out[s, p, at, :], hr[s, p, at, :]], axis=1)
        return pltpu.roll(line, lax.rem(wide - start, wide), axis=1)[:, :n]

    def take_rows(field, part, start, height):
        strips = [field[part, q, pl.ds(start, height), :] for q in range(n // LANES)]
        return jnp.concatenate(strips, axis=1)

    def put_rows(field, part, rows, value):
        for q in range(n // LANES):
            field[part, q, rows, :] = value[:, q * LANES : (q + 1) * LANES]

    size = H // PARTS
    chunks = [(p, h) for p in range(2) for h in range(PARTS)]
    lines = lambda h: pl.ds(h * size, size)

    outers = [
        {(p, h): copies.remote(xs.at[s, p, lines(h)], xr.at[s, p, lines(h)], has_outward, has_inward, outward) for p, h in chunks}
        for s in range(2)
    ]
    inners = [
        {(p, h): copies.remote(ss.at[s, p, lines(h)], sr.at[s, p, lines(h)], always, always, partner) for p, h in chunks}
        for s in range(2)
    ]
    for s in range(2):
        loads[s][0].wait()
        for c in halos[s][0]:
            c.arrived()
        for p, h in chunks:
            at = pl.ds(pl.multiple_of(odd * last + h * size, size), size)
            xs[s, p, lines(h)] = take_columns(s, p, at, far_col)
            outers[s][p, h].start()
    for s in range(2):
        loads[s][1].wait()
        for c in halos[s][1]:
            c.arrived()
        for p in range(2):
            ss[s, p] = take_columns(s, p, mate_rows, mate_col)

    mate_near = jnp.where(even, mate_row <= half, mate_row > half)

    def pass_on(s, i):
        p, h = chunks[i]
        outers[s][p, h].arrived()
        ss[s, p, lines(h)] = jnp.where(mate_near, ss[s, p, lines(h)], xr[s, p, lines(h)])
        inners[s][p, h].start()

    for c in load_small[:3]:
        c.wait()

    def propagator(lo, hi):
        @pl.loop(lo // LANES, hi // LANES)
        def _(i):
            at = pl.ds(pl.multiple_of(i * LANES, LANES), LANES)
            phase = k[0, at, :]
            k[1, at, :] = jnp.sin(phase)
            k[0, at, :] = jnp.cos(phase)

    def fill_body(s, p):
        for lo in (0, last):
            put_rows(bodies[s], p, slice(H + lo, 2 * H + lo), take_columns(s, p, slice(lo, lo + H), my_col))

        @pl.loop(0, (last - H) // H)
        def _(i):
            at = pl.ds(pl.multiple_of(H + i * H, H), H)
            to = pl.ds(pl.multiple_of(2 * H + i * H, H), H)
            put_rows(bodies[s], p, to, take_columns(s, p, at, my_col))

    def body_ready(s):
        loads[s][2].wait()
        for c in halos[s][2]:
            c.arrived()

    count = len(chunks)
    make_tables(cos, sin, fwd, bwd)
    pass_on(0, 0)
    propagator(0, n // 2)
    pass_on(0, 1)
    propagator(n // 2, n)
    body_ready(0)
    for i in range(2, count):
        pass_on(0, i)
        if i < 4:
            fill_body(0, i - 2)
    for c in load_small[3:]:
        c.wait()

    def halo_rows(s):
        for p, h in chunks:
            inners[s][p, h].arrived()
        for p in range(2):
            block = sr[s, p]
            put_rows(bodies[s], p, slice(0, H), block)
            put_rows(bodies[s], p, slice(tall - H, tall), block)

    window = lambda s, p, lo, height: take_rows(bodies[s], p, my_row + lo, height)
    full = lambda lo, height: (pl.ds(lo, height), pl.ds(n + lo, height))

    def stage_one(left, between=()):
        for i in range(2):
            mid[:, i * n : (i + 1) * n] = jnp.dot(
                left[i * n : (i + 1) * n, :], src[...], preferred_element_type=F32
            ).astype(BF16)
            for f in between[i : i + 1]:
                f()

    def stage_two(right, spans, epilogue):
        rows = [mid[lo : lo + height, :] for lo, height in spans]
        rows = rows[0] if len(rows) == 1 else jnp.concatenate(rows, axis=0)
        result = jnp.dot(rows, right[...], preferred_element_type=F32)
        at = 0
        for lo, height in spans:
            epilogue(lo, height, result[at : at + height, :n], result[at : at + height, n:])
            at += height

    whole = [(0, n)]
    ends = [(0, H), (n - H, H)]
    middle = [(H, n - 2 * H)]

    halo_rows(0)
    pass_on(1, 0)

    @pl.loop(0, n // H)
    def _(i):
        at = pl.ds(pl.multiple_of(i * H, H), H)
        low = pl.ds(pl.multiple_of(n + i * H, H), H)
        a_re = window(0, 0, i * H, H)
        a_im = window(0, 1, i * H, H)
        q_re, q_im = probe[0, at, :], probe[1, at, :]
        src[at, :] = (q_re * a_re - q_im * a_im).astype(BF16)
        src[low, :] = (q_re * a_im + q_im * a_re).astype(BF16)

    def propagate(lo, height, re, im):
        at, low = full(lo, height)
        k_re, k_im = k[0, at, :], k[1, at, :]
        src[at, :] = (re * k_re - im * k_im).astype(BF16)
        src[low, :] = (re * k_im + im * k_re).astype(BF16)

    def keep(lo, height, re, im):
        at, _ = full(lo, height)
        psi[0, at, :] = re
        psi[1, at, :] = im

    stage_one(fwd, (lambda: pass_on(1, 1),))
    stage_two(bwd, whole, propagate)
    for i in range(2, count // 2 + 1):
        pass_on(1, i)
    stage_one(bwd)
    body_ready(1)
    fill_body(1, 0)
    for i in range(count // 2 + 1, count):
        pass_on(1, i)
    stage_two(fwd, whole, keep)
    fill_body(1, 1)

    halo_rows(1)

    @pl.loop(0, n // H)
    def _(i):
        at = pl.ds(pl.multiple_of(i * H, H), H)
        low = pl.ds(pl.multiple_of(n + i * H, H), H)
        b_re = window(1, 0, i * H, H)
        b_im = window(1, 1, i * H, H)
        p_re, p_im = psi[0, at, :], psi[1, at, :]
        src[at, :] = (p_re * b_re - p_im * b_im).astype(BF16)
        src[low, :] = (p_re * b_im + p_im * b_re).astype(BF16)

    def detect(lo, height, re, im):
        at, low = full(lo, height)
        factor = 1.0 - amp[at, :].astype(F32) / jnp.sqrt(re * re + im * im + 1.0)
        src[at, :] = (re * factor).astype(BF16)
        src[low, :] = (im * factor).astype(BF16)

    def emit(s, p, lo, height, value):
        put_rows(gzs[s], p, pl.ds(first_row + lo, height), value)
        lane = lax.broadcasted_iota(jnp.int32, (height, LANES), 1)
        turn = lax.rem(my_col, LANES)
        at = pl.ds(lo, height)
        own_l[s, p, at, :] = jnp.where(lane >= my_col, pltpu.roll(value[:, :LANES], turn, axis=1), 0.0)
        own_r[s, p, at, :] = jnp.where(
            lane < my_col - (inner + H - n), pltpu.roll(value[:, n - LANES :], turn, axis=1), 0.0
        )

    def spread(lo, height, re, im):
        at, low = full(lo, height)
        p_re, p_im = psi[0, at, :], psi[1, at, :]
        b_re = window(1, 0, lo, height)
        b_im = window(1, 1, lo, height)
        emit(1, 0, lo, height, weight * (p_re * re + p_im * im))
        emit(1, 1, lo, height, weight * (p_re * im - p_im * re))
        src[at, :] = (b_re * re + b_im * im).astype(BF16)
        src[low, :] = (b_re * im - b_im * re).astype(BF16)

    spills = [
        {(p, h): copies.remote(ss.at[s, p, lines(h)], orr.at[s, p, lines(h)], always, always, partner) for p, h in chunks}
        for s in range(2)
    ]
    relays = [
        {(p, h): copies.remote(orr.at[s, p, lines(h)], ox.at[s, p, lines(h)], has_inward, has_outward, inward) for p, h in chunks}
        for s in range(2)
    ]
    early = [
        [
            to_left(own_l.at[s], grs[s].at[:, first_row : first_row + n, :]),
            to_right(own_r.at[s], gls[s].at[:, first_row : first_row + n, :]),
        ]
        for s in range(2)
    ]
    lates = [
        {
            (p, h): [
                to_left(xs.at[s, p, lines(h), : 2 * H], near_r.at[s, p, lines(h)]),
                to_right(xs.at[s, p, lines(h), 2 * H : 4 * H], near_l.at[s, p, lines(h)]),
            ]
            for p, h in chunks
        }
        for s in range(2)
    ]

    def spill(s):
        start = jnp.where(my_row <= half, first_row - my_row, first_row + tile_rows + H - my_row)
        for p, h in chunks:
            inners[s][p, h].sent()
            ss[s, p, lines(h)] = take_rows(gzs[s], p, start + h * size, size)
            spills[s][p, h].start()

    def relay(s, i):
        spills[s][chunks[i]].arrived()
        relays[s][chunks[i]].start()

    def back(lo, height, re, im):
        at, low = full(lo, height)
        k_re, k_im = k[0, at, :], k[1, at, :]
        src[at, :] = (re * k_re + im * k_im).astype(BF16)
        src[low, :] = (im * k_re - re * k_im).astype(BF16)

    def finish(lo, height, re, im):
        at, _ = full(lo, height)
        q_re, q_im = probe[0, at, :], probe[1, at, :]
        emit(0, 0, lo, height, weight * (q_re * re + q_im * im))
        emit(0, 1, lo, height, weight * (q_re * im - q_im * re))

    stage_one(fwd)
    stage_two(bwd, whole, detect)
    stage_one(bwd)
    stage_two(fwd, ends, spread)
    spill(1)
    stage_two(fwd, middle, spread)
    for c in early[1]:
        c.start()
    stage_one(fwd)
    relay(1, 0)
    stage_two(bwd, whole, back)
    for i in range(1, count // 2):
        relay(1, i)
    stage_one(bwd)
    stage_two(fwd, ends, finish)
    spill(0)
    stage_two(fwd, middle, finish)
    for c in early[0]:
        c.start()

    spread_out = lambda block, start: pltpu.roll(
        jnp.concatenate([block, jnp.zeros((block.shape[0], wide - n), F32)], axis=1), start, axis=1
    )

    def place_own(s, p):
        @pl.loop(0, tile_rows // H)
        def _(i):
            block = spread_out(take_rows(gzs[s], p, tall - n - my_row + i * H, H), my_col)
            at = pl.ds(pl.multiple_of(i * H, H), H)
            out[s, p, at, :] -= step_ref[s] * block[:, H : H + inner]

    def place_near(s, i):
        p, h = chunks[i]
        relays[s][p, h].arrived()
        outers[s][p, h].sent()
        for e, mine, start in (
            (0, jnp.logical_and(has_above, above_row > half), above_col),
            (1, jnp.logical_and(has_below, below_row <= half), below_col),
        ):
            outer = even if e == 0 else jnp.logical_not(even)
            block = jnp.where(outer, ox[s, p, lines(h)], orr[s, p, lines(h)])
            block = spread_out(jnp.where(mine, block, jnp.zeros_like(block)), start)
            xs[s, p, lines(h), e * H : (e + 1) * H] = block[:, :H]
            xs[s, p, lines(h), (2 + e) * H : (3 + e) * H] = block[:, H + inner :]
            at = pl.ds(e * last + h * size, size)
            out[s, p, at, :] -= step_ref[s] * block[:, H : H + inner]
        for c in lates[s][p, h]:
            c.start()

    def sides(s):
        for c in early[s]:
            c.arrived()
        for p in range(2):

            @pl.loop(0, tile_rows // H)
            def _(i, p=p):
                at = pl.ds(pl.multiple_of(i * H, H), H)
                from_left = gls[s][p, pl.ds(tall - n - left_row + i * H, H), :]
                from_right = grs[s][p, pl.ds(tall - n - right_row + i * H, H), :]
                out[s, p, at, :H] -= step_ref[s] * from_left
                out[s, p, at, inner - H :] -= step_ref[s] * from_right

    def corners(s, i):
        p, h = chunks[i]
        for c in lates[s][p, h]:
            c.arrived()
        for e in range(2):
            at = pl.ds(e * last + h * size, size)
            out[s, p, at, :H] -= step_ref[s] * near_l[s, p, lines(h), e * H : (e + 1) * H]
            out[s, p, at, inner - H :] -= step_ref[s] * near_r[s, p, lines(h), e * H : (e + 1) * H]

    for i in range(count // 2, count):
        relay(1, i)
    place_own(1, 0)
    place_own(1, 1)
    for i in range(count):
        place_near(1, i)
    relay(0, 0)
    place_own(0, 0)
    relay(0, 1)
    place_own(0, 1)
    sides(1)
    for i in range(2, count):
        relay(0, i)
        place_near(0, i - 2)
    for i in range(count):
        corners(1, i)
    sides(0)
    for i in range(count - 2, count):
        place_near(0, i)
    for i in range(count):
        corners(0, i)

    for c in copies.remotes:
        if not c.waited:
            c.sent()
    assert len(copies.remotes) == REMOTES and copies.local_used == LOCALS


def write_kernel(done, out, sems):
    copies = []
    for s in range(2):
        for p in range(2):
            copies.append(pltpu.make_async_copy(done.at[s, p], out.at[s, p], sems.at[2 * s + p]))
    for c in copies:
        c.start()
    for c in copies:
        c.wait()


def per_device(object_tiles, probe, prop_phase, amplitudes, offsets, counts, step_size):
    n = probe.shape[1]
    rows, inner = object_tiles.shape[2:]
    cos, sin = dft_table(n)
    tall = rows + 2 * H
    smem = pl.BlockSpec(memory_space=pltpu.SMEM)
    anywhere = pl.BlockSpec(memory_space=pl.ANY)
    on_chip = pl.BlockSpec(memory_space=pltpu.VMEM)
    vmem = lambda *shape, kind=F32: pltpu.VMEM(shape, kind)
    block = vmem(2, 2, H, n)
    long = 2 * tall - n - 2 * H
    scratch = (
        [vmem(2, SUBLANES, LANES, kind=jnp.int32), vmem(4, 2, SUBLANES, LANES, kind=jnp.int32)]
        + [vmem(2, n, n), vmem(2, n, n)]
        + [vmem(n, n, kind=BF16)] * 3
        + [vmem(2 * n, 2 * n, kind=BF16)] * 2
        + [vmem(2 * n, n, kind=BF16), vmem(n, 2 * n, kind=BF16), vmem(2, n, n)]
        + [vmem(2, 2, rows, H)] * 2
        + [vmem(2, n // LANES, tall, LANES)] * 2
        + [block] * 4
        + [vmem(2, n // LANES, long, LANES)] * 2
        + [block] * 2
        + [vmem(2, 2, n, H)] * 2
        + [vmem(2, long, H)] * 4
        + [vmem(2, 2, H, 2 * H)] * 2
        + [pltpu.SemaphoreType.DMA((REMOTES,))] * 2
        + [pltpu.SemaphoreType.DMA((LOCALS,))]
    )
    done = pl.pallas_call(
        step_kernel,
        in_specs=[smem] * 3 + [anywhere] * 6,
        out_specs=on_chip,
        out_shape=pltpu.VMEM(object_tiles.shape, F32),
        scratch_shapes=scratch,
        name="step",
        compiler_params=pltpu.CompilerParams(
            collective_id=0, has_side_effects=True, vmem_limit_bytes=VMEM_LIMIT
        ),
    )(offsets[0, 0, 0], counts[0], step_size, object_tiles, probe, prop_phase, amplitudes, cos, sin)
    return pl.pallas_call(
        write_kernel,
        in_specs=[on_chip],
        out_specs=anywhere,
        out_shape=jax.ShapeDtypeStruct(object_tiles.shape, F32),
        scratch_shapes=[pltpu.SemaphoreType.DMA((4,))],
        name="write",
        compiler_params=pltpu.CompilerParams(vmem_limit_bytes=1 << 20),
    )(done)


VMEM_LIMIT = 54 << 20


def solution(mesh):
    return jax.shard_map(
        per_device,
        mesh=mesh,
        in_specs=(
            P(None, None, "rows", "cols"),
            P(),
            P(),
            P("rows", "cols", None, None, None),
            P("rows", "cols", None, None),
            P("rows", "cols"),
            P(),
        ),
        out_specs=P(None, None, "rows", "cols"),
        check_vma=False,
    )
```

```python
import math

import jax
import jax.numpy as jnp
import numpy as np
from jax import lax
from jax.experimental import pallas as pl
from jax.experimental.pallas import tpu as pltpu
from jax.sharding import PartitionSpec as P

H = 128
LANES = 128
SUBLANES = 8
EVEN_CHUNKS = [(p, h, H // 2) for p in range(2) for h in (0, H // 2)]
FIRST_SMALL = [(0, 0, H // 4), (0, H // 4, H // 4)] + EVEN_CHUNKS[1:]
LAST_SMALL = EVEN_CHUNKS[:3] + [(1, H // 2, H // 4), (1, 3 * H // 4, H // 4)]
FORWARD = (FIRST_SMALL, EVEN_CHUNKS)
BACKWARD = (LAST_SMALL, EVEN_CHUNKS)
F32 = jnp.float32
BF16 = jnp.bfloat16
MESH = pl.DeviceIdType.MESH


def dft_table(length):
    index = np.arange(length, dtype=np.int64)
    angles = ((index[:, None] * index[None, :]) % length).astype(np.float32) * np.float32(
        2.0 * math.pi / length
    )
    scaling = np.float32(1.0 / math.sqrt(length))
    return (
        jnp.asarray((np.cos(angles) * scaling).astype(BF16)),
        jnp.asarray((-np.sin(angles) * scaling).astype(BF16)),
    )


def make_tables(cos_ref, sin_ref, fwd, bwd):
    n = cos_ref.shape[0]
    c, s = cos_ref[...], sin_ref[...]
    for table, sine in ((fwd, s), (bwd, -s)):
        table[:n, :n] = c
        table[n:, n:] = c
        table[n:, :n] = sine
        table[:n, n:] = -sine


class Copies:
    def __init__(self, sends, receives, locals_):
        self.sends, self.receives, self.locals = sends, receives, locals_
        self.remotes = []
        self.local_used = 0

    def remote(self, src, dst, there, here, device):
        k = len(self.remotes)
        copy = pltpu.make_async_remote_copy(
            src_ref=src,
            dst_ref=dst,
            send_sem=self.sends.at[k],
            recv_sem=self.receives.at[k],
            device_id=device,
            device_id_type=MESH,
        )
        self.remotes.append(Remote(copy, there, here))
        return self.remotes[-1]

    def local(self, src, dst):
        k = self.local_used
        self.local_used += 1
        return pltpu.make_async_copy(src, dst, self.locals.at[k])


class Remote:
    def __init__(self, copy, there, here):
        self.copy, self.there, self.here = copy, there, here
        self.waited = False

    def start(self):
        pl.when(self.there)(lambda: self.copy.start())

    def arrived(self):
        pl.when(self.here)(lambda: self.copy.wait_recv())

    def sent(self):
        self.waited = True
        pl.when(self.there)(lambda: self.copy.wait_send())


REMOTES = 22 + 2 * sum(map(len, FORWARD)) + 4 * sum(map(len, BACKWARD))
LOCALS = 5 + 2 * 3


def step_kernel(
    offs_ref, count_ref, step_ref, obj, probe_in, phase_in, amp_in, cos_in, sin_in, out,
    meta, near, probe, k, amp, cos, sin, fwd, bwd, src, mid, psi,
    hl, hr, body0, body1, xs, xr, ss, sr, placed, ends_raw, share,
    orr, ox, own_l, own_r, gl0, gl1, gr0, gr1, near_l, near_r,
    sends, receives, locals_,
):
    n = cos.shape[0]
    tile_rows, inner = obj.shape[2:]
    wide = inner + 2 * H
    tall = tile_rows + 2 * H
    half = (tall - n) // 2
    last = tile_rows - H
    bodies, gls, grs = (body0, body1), (gl0, gl1), (gr0, gr1)

    me_r, me_c = lax.axis_index("rows"), lax.axis_index("cols")
    n_r, n_c = lax.axis_size("rows"), lax.axis_size("cols")
    odd = lax.rem(me_r, 2)
    even = odd == 0
    side = 1 - 2 * odd
    has_left, has_right = me_c > 0, me_c < n_c - 1
    has_above, has_below = me_r > 0, me_r < n_r - 1
    far_above, far_below = me_r > 1, me_r < n_r - 2
    row = lambda r: {"rows": r, "cols": me_c}
    col = lambda c: {"rows": me_r, "cols": c}
    partner = row(me_r + side)
    outward = row(me_r - 2 * side)
    inward = row(me_r + 2 * side)
    has_outward = jnp.where(even, me_r - 2, n_r - 3 - me_r) >= 0
    has_inward = jnp.where(even, n_r - 3 - me_r, me_r - 2) >= 0
    always = me_r >= 0

    copies = Copies(sends, receives, locals_)
    far_rows = pl.ds(pl.multiple_of(odd * last, H), H)
    mate_rows = pl.ds(pl.multiple_of((1 - odd) * last, H), H)
    mid_rows = pl.ds(H, last - H)
    pieces = (far_rows, mate_rows, mid_rows)

    loads = [[copies.local(obj.at[s, :, at, :], out.at[s, :, at, :]) for at in pieces] for s in range(2)]
    load_small = [
        copies.local(a, b)
        for a, b in ((cos_in, cos), (sin_in, sin), (phase_in, k.at[0]), (probe_in, probe), (amp_in.at[0, 0, 0], amp))
    ]
    for c in loads[0][:2] + loads[1][:2] + load_small[:3] + loads[0][2:] + load_small[3:] + loads[1][2:]:
        c.start()
    for i in range(2):
        meta[i] = jnp.full(meta.shape[1:], offs_ref[i], jnp.int32)

    barrier = pltpu.get_barrier_semaphore()
    greeted = (
        (has_left, col(me_c - 1)), (has_right, col(me_c + 1)),
        (has_above, row(me_r - 1)), (has_below, row(me_r + 1)),
        (far_above, row(me_r - 2)), (far_below, row(me_r + 2)),
    )
    total = jnp.int32(0)
    for exists, device in greeted:
        total += exists.astype(jnp.int32)

        @pl.when(exists)
        def _(device=device):
            pl.semaphore_signal(barrier, inc=1, device_id=device, device_id_type=MESH)

    first_row = tall - n - H

    @pl.when(jnp.logical_not(has_left))
    def _():
        hl[...] = jnp.zeros_like(hl)
        near_l[...] = jnp.zeros_like(near_l)
        for ref in gls:
            ref[:, first_row : first_row + n, :] = jnp.zeros((2, n, H), F32)

    @pl.when(jnp.logical_not(has_right))
    def _():
        hr[...] = jnp.zeros_like(hr)
        near_r[...] = jnp.zeros_like(near_r)
        for ref in grs:
            ref[:, first_row : first_row + n, :] = jnp.zeros((2, n, H), F32)

    @pl.when(jnp.logical_not(has_inward))
    def _():
        xr[...] = jnp.zeros_like(xr)

    @pl.when(jnp.logical_not(has_outward))
    def _():
        ox[...] = jnp.zeros_like(ox)

    for i, exists in enumerate((has_above, has_below, has_left, has_right)):

        @pl.when(jnp.logical_not(exists))
        def _(i=i):
            near[i] = jnp.zeros(near.shape[1:], jnp.int32)

    pl.semaphore_wait(barrier, total)

    to_right = lambda a, b: copies.remote(a, b, has_right, has_left, col(me_c + 1))
    to_left = lambda a, b: copies.remote(a, b, has_left, has_right, col(me_c - 1))
    metas = [
        copies.remote(meta, near.at[0], has_below, has_above, row(me_r + 1)),
        copies.remote(meta, near.at[1], has_above, has_below, row(me_r - 1)),
        to_right(meta, near.at[2]),
        to_left(meta, near.at[3]),
    ]
    def halo(s, at, p=slice(None)):
        return [
            to_right(obj.at[s, p, at, inner - H :], hl.at[s, p, at, :]),
            to_left(obj.at[s, p, at, 0:H], hr.at[s, p, at, :]),
        ]

    halos = [[halo(s, at) for at in pieces] if s else [None] + [halo(s, at) for at in pieces[1:]] for s in range(2)]
    halo_first = [halo(0, far_rows, p) for p in range(2)]
    halos[0][0] = halo_first[0] + halo_first[1]
    for group in (metas, halos[0][0], halos[0][1], halos[1][0], halos[1][1], halos[0][2], halos[1][2]):
        for c in group:
            c.start()

    tiles = n // LANES + 1
    long = placed.shape[1]

    @pl.loop(0, 2 * tiles)
    def _(q):
        placed[q, :first_row, :] = jnp.zeros((first_row, LANES), F32)
        placed[q, first_row + n :, :] = jnp.zeros((first_row, LANES), F32)

    placed[2 * tiles] = jnp.zeros((long, LANES), F32)
    for lo, hi in ((0, first_row), (first_row + n, long)):
        for ref in gls + grs:
            ref[:, lo:hi, :] = jnp.zeros((2, hi - lo, H), F32)
    for lo in (0, 3 * H):
        ends_raw[:, :, lo : lo + H, :] = jnp.zeros((2, n // LANES, H, LANES), F32)

    my_row, my_col = offs_ref[0], offs_ref[1]
    weight = jnp.where(count_ref[0] > 0, 1.0, 0.0).astype(F32)
    for c in metas:
        c.arrived()
    above_row, above_col = jnp.max(near[0, 0]), jnp.max(near[0, 1])
    below_row, below_col = jnp.max(near[1, 0]), jnp.max(near[1, 1])
    left_row, right_row = jnp.max(near[2, 0]), jnp.max(near[3, 0])
    mate_row = jnp.where(even, below_row, above_row)
    mate_col = jnp.where(even, below_col, above_col)
    far_col = jnp.where(even, above_col, below_col)

    def take_columns(s, p, at, start):
        line = jnp.concatenate([hl[s, p, at, :], out[s, p, at, :], hr[s, p, at, :]], axis=1)
        return pltpu.roll(line, lax.rem(wide - start, wide), axis=1)[:, :n]

    def take_rows(field, part, start, height):
        strips = [field[part, q, pl.ds(start, height), :] for q in range(n // LANES)]
        return jnp.concatenate(strips, axis=1)

    def put_rows(field, part, rows, value):
        for q in range(n // LANES):
            field[part, q, rows, :] = value[:, q * LANES : (q + 1) * LANES]

    along = lambda chunks, source, target, there, here, device: [
        copies.remote(source.at[p, pl.ds(h, size)], target.at[p, pl.ds(h, size)], there, here, device)
        for p, h, size in chunks
    ]
    outers = [along(FORWARD[s], xs.at[s], xr.at[s], has_outward, has_inward, outward) for s in range(2)]
    inners = [along(FORWARD[s], ss.at[s], sr.at[s], always, always, partner) for s in range(2)]
    for s in range(2):
        loads[s][0].wait()
        if s:
            for c in halos[s][0]:
                c.arrived()
        for i, (p, h, size) in enumerate(FORWARD[s]):
            if not s and h == 0:
                for c in halo_first[p]:
                    c.arrived()
            at = pl.ds(pl.multiple_of(odd * last + h, SUBLANES), size)
            xs[s, p, pl.ds(h, size)] = take_columns(s, p, at, far_col)
            outers[s][i].start()
    for s in range(2):
        loads[s][1].wait()
        for c in halos[s][1]:
            c.arrived()
        for p in range(2):
            ss[s, p] = take_columns(s, p, mate_rows, mate_col)

    mate_near = jnp.where(even, mate_row <= half, mate_row > half)

    def pass_on(s, *which):
        for i in which:
            p, h, size = FORWARD[s][i]
            at = pl.ds(h, size)
            outers[s][i].arrived()
            ss[s, p, at] = jnp.where(mate_near, ss[s, p, at], xr[s, p, at])
            inners[s][i].start()

    for c in load_small[:3]:
        c.wait()

    def propagator(lo, hi):
        @pl.loop(lo // LANES, hi // LANES)
        def _(i):
            at = pl.ds(pl.multiple_of(i * LANES, LANES), LANES)
            phase = k[0, at, :]
            k[1, at, :] = jnp.sin(phase)
            k[0, at, :] = jnp.cos(phase)

    def fill_body(s, p):
        for lo in (0, last):
            put_rows(bodies[s], p, slice(H + lo, 2 * H + lo), take_columns(s, p, slice(lo, lo + H), my_col))

        @pl.loop(0, (last - H) // H)
        def _(i):
            at = pl.ds(pl.multiple_of(H + i * H, H), H)
            to = pl.ds(pl.multiple_of(2 * H + i * H, H), H)
            put_rows(bodies[s], p, to, take_columns(s, p, at, my_col))

    def body_ready(s):
        loads[s][2].wait()
        for c in halos[s][2]:
            c.arrived()

    pass_on(0, 0)
    make_tables(cos, sin, fwd, bwd)
    pass_on(0, 1)
    propagator(0, n // 2)
    pass_on(0, 2)
    propagator(n // 2, n)
    pass_on(0, 3)
    body_ready(0)
    fill_body(0, 0)
    pass_on(0, 4)
    fill_body(0, 1)
    for c in load_small[3:]:
        c.wait()

    def halo_rows(s):
        for c in inners[s]:
            c.arrived()
        for p in range(2):
            block = sr[s, p]
            put_rows(bodies[s], p, slice(0, H), block)
            put_rows(bodies[s], p, slice(tall - H, tall), block)

    window = lambda s, p, lo, height: take_rows(bodies[s], p, my_row + lo, height)
    full = lambda lo, height: (pl.ds(lo, height), pl.ds(n + lo, height))

    def stage_one(left, between=()):
        for i in range(2):
            mid[:, i * n : (i + 1) * n] = jnp.dot(
                left[i * n : (i + 1) * n, :], src[...], preferred_element_type=F32
            ).astype(BF16)
            for f in between[i : i + 1]:
                f()

    interior = ((H, n - H), (n + H, 2 * n - H))
    exterior = ((0, H), (n - H, n + H), (2 * n - H, 2 * n))

    def product(left, i, spans):
        rows = slice(i * n, (i + 1) * n)
        return jnp.dot(
            jnp.concatenate([left[rows, a:b] for a, b in spans], axis=1),
            jnp.concatenate([src[a:b, :] for a, b in spans], axis=0),
            preferred_element_type=F32,
        )

    def stage_two(right, spans, epilogue):
        rows = [mid[lo : lo + height, :] for lo, height in spans]
        rows = rows[0] if len(rows) == 1 else jnp.concatenate(rows, axis=0)
        result = jnp.dot(rows, right[...], preferred_element_type=F32)
        at = 0
        for lo, height in spans:
            epilogue(lo, height, result[at : at + height, :n], result[at : at + height, n:])
            at += height

    whole = [(0, n)]
    ends = [(0, H), (n - H, H)]
    middle = [(H, n - 2 * H)]

    halo_rows(0)
    pass_on(1, 0)

    @pl.loop(0, n // H)
    def _(i):
        at = pl.ds(pl.multiple_of(i * H, H), H)
        low = pl.ds(pl.multiple_of(n + i * H, H), H)
        a_re = window(0, 0, i * H, H)
        a_im = window(0, 1, i * H, H)
        q_re, q_im = probe[0, at, :], probe[1, at, :]
        src[at, :] = (q_re * a_re - q_im * a_im).astype(BF16)
        src[low, :] = (q_re * a_im + q_im * a_re).astype(BF16)

    def propagate(lo, height, re, im):
        at, low = full(lo, height)
        k_re, k_im = k[0, at, :], k[1, at, :]
        src[at, :] = (re * k_re - im * k_im).astype(BF16)
        src[low, :] = (re * k_im + im * k_re).astype(BF16)

    def keep(lo, height, re, im):
        at, _ = full(lo, height)
        psi[0, at, :] = re
        psi[1, at, :] = im

    def exit_wave(lo, height):
        at, low = full(lo, height)
        b_re = window(1, 0, lo, height)
        b_im = window(1, 1, lo, height)
        p_re, p_im = psi[0, at, :], psi[1, at, :]
        src[at, :] = (p_re * b_re - p_im * b_im).astype(BF16)
        src[low, :] = (p_re * b_im + p_im * b_re).astype(BF16)

    stage_one(fwd)
    stage_two(bwd, whole, propagate)
    pass_on(1, 1)
    stage_one(bwd)
    body_ready(1)
    fill_body(1, 0)
    pass_on(1, 2)
    stage_two(fwd, whole, keep)
    pass_on(1, 3)
    fill_body(1, 1)
    for lo in range(H, n - H, H):
        exit_wave(lo, H)
    for i in range(2):
        share[i] = product(fwd, i, interior)
    halo_rows(1)
    for lo in (0, n - H):
        exit_wave(lo, H)

    def detect(lo, height, re, im):
        at, low = full(lo, height)
        factor = 1.0 - amp[at, :].astype(F32) / jnp.sqrt(re * re + im * im + 1.0)
        src[at, :] = (re * factor).astype(BF16)
        src[low, :] = (im * factor).astype(BF16)

    turn = lax.rem(my_col, LANES)

    def emit(s, p, lo, height, value):
        lane = lax.broadcasted_iota(jnp.int32, (height, LANES), 1)
        zero = jnp.zeros((height, LANES), F32)
        pieces = [value[:, q * LANES : (q + 1) * LANES] for q in range(n // LANES)]
        turned = [pltpu.roll(piece, turn, axis=1) for piece in pieces]
        at = pl.ds(first_row + lo, height)
        for q in range(tiles):
            before = turned[q - 1] if q else zero
            here = turned[q] if q < tiles - 1 else zero
            placed[p * tiles + q, at, :] = jnp.where(lane >= turn, here, before)
        own_l[s, p, pl.ds(lo, height), :] = jnp.where(lane >= my_col, turned[0], 0.0)
        own_r[s, p, pl.ds(lo, height), :] = jnp.where(lane < my_col - (inner + H - n), turned[-1], 0.0)
        if (lo, height) in ends:
            for q, piece in enumerate(pieces):
                ends_raw[p, q, pl.ds(H if lo == 0 else 2 * H, H), :] = piece

    def spread(lo, height, re, im):
        at, low = full(lo, height)
        p_re, p_im = psi[0, at, :], psi[1, at, :]
        b_re = window(1, 0, lo, height)
        b_im = window(1, 1, lo, height)
        emit(1, 0, lo, height, weight * (p_re * re + p_im * im))
        emit(1, 1, lo, height, weight * (p_re * im - p_im * re))
        src[at, :] = (b_re * re + b_im * im).astype(BF16)
        src[low, :] = (b_re * im - b_im * re).astype(BF16)

    spills = [along(BACKWARD[s], ss.at[s], orr.at[s], always, always, partner) for s in range(2)]
    relays = [along(BACKWARD[s], orr.at[s], ox.at[s], has_inward, has_outward, inward) for s in range(2)]
    early = [
        [
            to_left(own_l.at[s], grs[s].at[:, first_row : first_row + n, :]),
            to_right(own_r.at[s], gls[s].at[:, first_row : first_row + n, :]),
        ]
        for s in range(2)
    ]
    lates = [
        [
            [
                to_left(xs.at[s, p, pl.ds(h, size), : 2 * H], near_r.at[s, p, pl.ds(h, size)]),
                to_right(xs.at[s, p, pl.ds(h, size), 2 * H : 4 * H], near_l.at[s, p, pl.ds(h, size)]),
            ]
            for p, h, size in BACKWARD[s]
        ]
        for s in range(2)
    ]

    def spill(s):
        lower = tile_rows + 4 * H - n - jnp.maximum(my_row, tall - n - H)
        start = jnp.where(my_row <= half, H - jnp.minimum(my_row, H), lower)
        for c in inners[s]:
            c.sent()
        for i, (p, h, size) in enumerate(BACKWARD[s]):
            ss[s, p, pl.ds(h, size)] = take_rows(ends_raw, p, start + h, size)
            spills[s][i].start()

    def relay(s, *which):
        for i in which:
            spills[s][i].arrived()
            relays[s][i].start()

    def back(lo, height, re, im):
        at, low = full(lo, height)
        k_re, k_im = k[0, at, :], k[1, at, :]
        src[at, :] = (re * k_re + im * k_im).astype(BF16)
        src[low, :] = (im * k_re - re * k_im).astype(BF16)

    def finish(lo, height, re, im):
        at, _ = full(lo, height)
        q_re, q_im = probe[0, at, :], probe[1, at, :]
        emit(0, 0, lo, height, weight * (q_re * re + q_im * im))
        emit(0, 1, lo, height, weight * (q_re * im - q_im * re))

    spread_out = lambda block, start: pltpu.roll(
        jnp.concatenate([block, jnp.zeros((block.shape[0], wide - n), F32)], axis=1), start, axis=1
    )

    column = sum(jnp.where(my_col >= q * LANES, 1, 0) for q in range(1, (wide - n) // LANES + 1))

    def place_own(s, p):
        @pl.loop(0, tile_rows // H)
        def _(i):
            at = pl.ds(pl.multiple_of(i * H, H), H)
            for j in range(inner // LANES):
                tile = j + H // LANES - column
                inside = jnp.logical_and(tile >= 0, tile < tiles)
                tile = jnp.where(inside, p * tiles + tile, 2 * tiles)
                block = placed[tile, pl.ds(tall - n - my_row + i * H, H), :]
                lanes = slice(j * LANES, (j + 1) * LANES)
                out[s, p, at, lanes] -= step_ref[s] * block

    def place_near(s, i):
        p, h, size = BACKWARD[s][i]
        at = pl.ds(h, size)
        relays[s][i].arrived()
        for e, mine, start in (
            (0, jnp.logical_and(has_above, above_row > half), above_col),
            (1, jnp.logical_and(has_below, below_row <= half), below_col),
        ):
            outer = even if e == 0 else jnp.logical_not(even)
            block = jnp.where(outer, ox[s, p, at], orr[s, p, at])
            block = spread_out(jnp.where(mine, block, jnp.zeros_like(block)), start)
            xs[s, p, at, e * H : (e + 1) * H] = block[:, :H]
            xs[s, p, at, (2 + e) * H : (3 + e) * H] = block[:, H + inner :]
            rows = pl.ds(e * last + h, size)
            out[s, p, rows, :] -= step_ref[s] * block[:, H : H + inner]
        for c in lates[s][i]:
            c.start()

    def sides(s):
        for c in early[s]:
            c.arrived()
        for p in range(2):

            @pl.loop(0, tile_rows // H)
            def _(i, p=p):
                at = pl.ds(pl.multiple_of(i * H, H), H)
                from_left = gls[s][p, pl.ds(tall - n - left_row + i * H, H), :]
                from_right = grs[s][p, pl.ds(tall - n - right_row + i * H, H), :]
                out[s, p, at, :H] -= step_ref[s] * from_left
                out[s, p, at, inner - H :] -= step_ref[s] * from_right

    def corners(s, i):
        p, h, size = BACKWARD[s][i]
        for c in lates[s][i]:
            c.arrived()
        for e in range(2):
            at = pl.ds(e * last + h, size)
            out[s, p, at, :H] -= step_ref[s] * near_l[s, p, pl.ds(h, size), e * H : (e + 1) * H]
            out[s, p, at, inner - H :] -= step_ref[s] * near_r[s, p, pl.ds(h, size), e * H : (e + 1) * H]

    for i in range(2):
        mid[:, i * n : (i + 1) * n] = (share[i] + product(fwd, i, exterior)).astype(BF16)
    stage_two(bwd, whole, detect)
    stage_one(bwd)
    stage_two(fwd, ends, spread)
    spill(1)
    stage_two(fwd, middle, spread)
    for c in early[1]:
        c.start()
    stage_one(fwd)
    relay(1, 0)
    stage_two(bwd, whole, back)
    place_own(1, 0)
    relay(1, 1)
    place_own(1, 1)
    stage_one(bwd)
    stage_two(fwd, ends, finish)
    spill(0)
    relay(1, 2)
    stage_two(fwd, middle, finish)
    for c in early[0]:
        c.start()
    for c in outers[0] + outers[1]:
        c.sent()
    relay(1, 3)
    place_near(1, 0)
    place_near(1, 1)
    place_own(0, 0)
    relay(0, 0)
    place_near(1, 2)
    place_near(1, 3)
    place_own(0, 1)
    relay(0, 1)
    sides(1)
    relay(0, 2)
    for i in range(4):
        corners(1, i)
    place_near(0, 0)
    relay(0, 3)
    place_near(0, 1)
    relay(0, 4)
    sides(0)
    for i in range(2, 5):
        place_near(0, i)
    for i in range(5):
        corners(0, i)

    for c in copies.remotes:
        if not c.waited:
            c.sent()
    assert len(copies.remotes) == REMOTES and copies.local_used == LOCALS


def write_kernel(done, out, sems):
    copies = []
    rows = done.shape[2] // 3
    for i in range(12):
        at = (i // 6, i // 3 % 2, pl.ds(i % 3 * rows, rows))
        copies.append(pltpu.make_async_copy(done.at[at], out.at[at], sems.at[i]))
    for c in copies:
        c.start()
    for c in copies:
        c.wait()


def per_device(object_tiles, probe, prop_phase, amplitudes, offsets, counts, step_size):
    n = probe.shape[1]
    rows, inner = object_tiles.shape[2:]
    cos, sin = dft_table(n)
    tall = rows + 2 * H
    smem = pl.BlockSpec(memory_space=pltpu.SMEM)
    anywhere = pl.BlockSpec(memory_space=pl.ANY)
    on_chip = pl.BlockSpec(memory_space=pltpu.VMEM)
    vmem = lambda *shape, kind=F32: pltpu.VMEM(shape, kind)
    block = vmem(2, 2, H, n)
    long = 2 * tall - n - 2 * H
    scratch = (
        [vmem(2, SUBLANES, LANES, kind=jnp.int32), vmem(4, 2, SUBLANES, LANES, kind=jnp.int32)]
        + [vmem(2, n, n), vmem(2, n, n)]
        + [vmem(n, n, kind=BF16)] * 3
        + [vmem(2 * n, 2 * n, kind=BF16)] * 2
        + [vmem(2 * n, n, kind=BF16), vmem(n, 2 * n, kind=BF16), vmem(2, n, n)]
        + [vmem(2, 2, rows, H)] * 2
        + [vmem(2, n // LANES, tall, LANES)] * 2
        + [block] * 4
        + [vmem(2 * (n // LANES + 1) + 1, long, LANES), vmem(2, n // LANES, 4 * H, LANES), vmem(2, n, n)]
        + [block] * 2
        + [vmem(2, 2, n, H)] * 2
        + [vmem(2, long, H)] * 4
        + [vmem(2, 2, H, 2 * H)] * 2
        + [pltpu.SemaphoreType.DMA((REMOTES,))] * 2
        + [pltpu.SemaphoreType.DMA((LOCALS,))]
    )
    done = pl.pallas_call(
        step_kernel,
        in_specs=[smem] * 3 + [anywhere] * 6,
        out_specs=on_chip,
        out_shape=pltpu.VMEM(object_tiles.shape, F32),
        scratch_shapes=scratch,
        name="step",
        compiler_params=pltpu.CompilerParams(
            collective_id=0, has_side_effects=True, vmem_limit_bytes=VMEM_LIMIT
        ),
    )(offsets[0, 0, 0], counts[0], step_size, object_tiles, probe, prop_phase, amplitudes, cos, sin)
    return pl.pallas_call(
        write_kernel,
        in_specs=[on_chip],
        out_specs=anywhere,
        out_shape=jax.ShapeDtypeStruct(object_tiles.shape, F32),
        scratch_shapes=[pltpu.SemaphoreType.DMA((12,))],
        name="write",
        compiler_params=pltpu.CompilerParams(vmem_limit_bytes=1 << 20),
    )(done)


VMEM_LIMIT = 54 << 20


def solution(mesh):
    return jax.shard_map(
        per_device,
        mesh=mesh,
        in_specs=(
            P(None, None, "rows", "cols"),
            P(),
            P(),
            P("rows", "cols", None, None, None),
            P("rows", "cols", None, None),
            P("rows", "cols"),
            P(),
        ),
        out_specs=P(None, None, "rows", "cols"),
        check_vma=False,
    )
```

```python
import math

import jax
import jax.numpy as jnp
import numpy as np
from jax import lax
from jax.experimental import pallas as pl
from jax.experimental.pallas import tpu as pltpu
from jax.sharding import PartitionSpec as P

H = 128
LANES = 128
SUBLANES = 8
EVEN_CHUNKS = [(p, h, H // 2) for p in range(2) for h in (0, H // 2)]
LAST_SMALL = EVEN_CHUNKS[:3] + [(1, H // 2, H // 4), (1, 3 * H // 4, H // 8), (1, 7 * H // 8, H // 8)]
FORWARD = (EVEN_CHUNKS[:3] + [(1, H // 2, H // 4), (1, 3 * H // 4, H // 4)], LAST_SMALL)
BACKWARD = (LAST_SMALL, EVEN_CHUNKS)
F32 = jnp.float32
BF16 = jnp.bfloat16
MESH = pl.DeviceIdType.MESH


def dft_table(length):
    index = np.arange(length, dtype=np.int64)
    angles = ((index[:, None] * index[None, :]) % length).astype(np.float32) * np.float32(
        2.0 * math.pi / length
    )
    scaling = np.float32(1.0 / math.sqrt(length))
    return (
        jnp.asarray((np.cos(angles) * scaling).astype(BF16)),
        jnp.asarray((-np.sin(angles) * scaling).astype(BF16)),
    )


def make_tables(cos_ref, sin_ref, fwd, bwd):
    n = cos_ref.shape[0]
    c, s = cos_ref[...], sin_ref[...]
    for table, sine in ((fwd, s), (bwd, -s)):
        table[:n, :n] = c
        table[n:, n:] = c
        table[n:, :n] = sine
        table[:n, n:] = -sine


class Copies:
    def __init__(self, sends, receives, locals_):
        self.sends, self.receives, self.locals = sends, receives, locals_
        self.remotes = []
        self.local_used = 0

    def remote(self, src, dst, there, here, device):
        k = len(self.remotes)
        copy = pltpu.make_async_remote_copy(
            src_ref=src,
            dst_ref=dst,
            send_sem=self.sends.at[k],
            recv_sem=self.receives.at[k],
            device_id=device,
            device_id_type=MESH,
        )
        self.remotes.append(Remote(copy, there, here))
        return self.remotes[-1]

    def local(self, src, dst):
        k = self.local_used
        self.local_used += 1
        return pltpu.make_async_copy(src, dst, self.locals.at[k])


class Remote:
    def __init__(self, copy, there, here):
        self.copy, self.there, self.here = copy, there, here
        self.waited = False

    def start(self):
        pl.when(self.there)(lambda: self.copy.start())

    def arrived(self):
        pl.when(self.here)(lambda: self.copy.wait_recv())

    def sent(self):
        self.waited = True
        pl.when(self.there)(lambda: self.copy.wait_send())


REMOTES = 22 + 2 * sum(map(len, FORWARD)) + 4 * sum(map(len, BACKWARD))
LOCALS = 5 + 2 * 3


def step_kernel(
    offs_ref, count_ref, step_ref, obj, probe_in, phase_in, amp_in, cos_in, sin_in, out,
    meta, near, probe, k, amp, cos, sin, fwd, bwd, src, mid, psi,
    hl, hr, body0, body1, xs, xr, ss, sr, placed, ends_raw, share,
    orr, ox, own_l, own_r, gl0, gl1, gr0, gr1, near_l, near_r,
    sends, receives, locals_,
):
    n = cos.shape[0]
    tile_rows, inner = obj.shape[2:]
    wide = inner + 2 * H
    tall = tile_rows + 2 * H
    half = (tall - n) // 2
    last = tile_rows - H
    bodies, gls, grs = (body0, body1), (gl0, gl1), (gr0, gr1)

    me_r, me_c = lax.axis_index("rows"), lax.axis_index("cols")
    n_r, n_c = lax.axis_size("rows"), lax.axis_size("cols")
    odd = lax.rem(me_r, 2)
    even = odd == 0
    side = 1 - 2 * odd
    has_left, has_right = me_c > 0, me_c < n_c - 1
    has_above, has_below = me_r > 0, me_r < n_r - 1
    far_above, far_below = me_r > 1, me_r < n_r - 2
    row = lambda r: {"rows": r, "cols": me_c}
    col = lambda c: {"rows": me_r, "cols": c}
    partner = row(me_r + side)
    outward = row(me_r - 2 * side)
    inward = row(me_r + 2 * side)
    has_outward = jnp.where(even, me_r - 2, n_r - 3 - me_r) >= 0
    has_inward = jnp.where(even, n_r - 3 - me_r, me_r - 2) >= 0
    always = me_r >= 0

    copies = Copies(sends, receives, locals_)
    far_rows = pl.ds(pl.multiple_of(odd * last, H), H)
    mate_rows = pl.ds(pl.multiple_of((1 - odd) * last, H), H)
    mid_rows = pl.ds(H, last - H)
    pieces = (far_rows, mate_rows, mid_rows)

    loads = [[copies.local(obj.at[s, :, at, :], out.at[s, :, at, :]) for at in pieces] for s in range(2)]
    load_small = [
        copies.local(a, b)
        for a, b in ((cos_in, cos), (sin_in, sin), (phase_in, k.at[0]), (probe_in, probe), (amp_in.at[0, 0, 0], amp))
    ]
    for c in loads[0][:2] + loads[1][:2] + load_small[:3] + loads[0][2:] + load_small[3:] + loads[1][2:]:
        c.start()
    for i in range(2):
        meta[i] = jnp.full(meta.shape[1:], offs_ref[i], jnp.int32)

    barrier = pltpu.get_barrier_semaphore()
    greeted = (
        (has_left, col(me_c - 1)), (has_right, col(me_c + 1)),
        (has_above, row(me_r - 1)), (has_below, row(me_r + 1)),
        (far_above, row(me_r - 2)), (far_below, row(me_r + 2)),
    )
    total = jnp.int32(0)
    for exists, device in greeted:
        total += exists.astype(jnp.int32)

        @pl.when(exists)
        def _(device=device):
            pl.semaphore_signal(barrier, inc=1, device_id=device, device_id_type=MESH)

    first_row = tall - n - H

    @pl.when(jnp.logical_not(has_left))
    def _():
        hl[...] = jnp.zeros_like(hl)
        near_l[...] = jnp.zeros_like(near_l)
        for ref in gls:
            ref[:, first_row : first_row + n, :] = jnp.zeros((2, n, H), F32)

    @pl.when(jnp.logical_not(has_right))
    def _():
        hr[...] = jnp.zeros_like(hr)
        near_r[...] = jnp.zeros_like(near_r)
        for ref in grs:
            ref[:, first_row : first_row + n, :] = jnp.zeros((2, n, H), F32)

    @pl.when(jnp.logical_not(has_inward))
    def _():
        xr[...] = jnp.zeros_like(xr)

    @pl.when(jnp.logical_not(has_outward))
    def _():
        ox[...] = jnp.zeros_like(ox)

    for i, exists in enumerate((has_above, has_below, has_left, has_right)):

        @pl.when(jnp.logical_not(exists))
        def _(i=i):
            near[i] = jnp.zeros(near.shape[1:], jnp.int32)

    pl.semaphore_wait(barrier, total)

    to_right = lambda a, b: copies.remote(a, b, has_right, has_left, col(me_c + 1))
    to_left = lambda a, b: copies.remote(a, b, has_left, has_right, col(me_c - 1))
    metas = [
        copies.remote(meta, near.at[0], has_below, has_above, row(me_r + 1)),
        copies.remote(meta, near.at[1], has_above, has_below, row(me_r - 1)),
        to_right(meta, near.at[2]),
        to_left(meta, near.at[3]),
    ]
    def halo(s, at, p=slice(None)):
        return [
            to_right(obj.at[s, p, at, inner - H :], hl.at[s, p, at, :]),
            to_left(obj.at[s, p, at, 0:H], hr.at[s, p, at, :]),
        ]

    halos = [[halo(s, at) for at in pieces] if s else [None] + [halo(s, at) for at in pieces[1:]] for s in range(2)]
    halo_first = [halo(0, far_rows, p) for p in range(2)]
    halos[0][0] = halo_first[0] + halo_first[1]
    for group in (metas, halos[0][0], halos[0][1], halos[1][0], halos[1][1], halos[0][2], halos[1][2]):
        for c in group:
            c.start()

    tiles = n // LANES + 1
    long = placed.shape[1]

    @pl.loop(0, 2 * tiles)
    def _(q):
        placed[q, :first_row, :] = jnp.zeros((first_row, LANES), F32)
        placed[q, first_row + n :, :] = jnp.zeros((first_row, LANES), F32)

    placed[2 * tiles] = jnp.zeros((long, LANES), F32)
    for lo, hi in ((0, first_row), (first_row + n, long)):
        for ref in gls + grs:
            ref[:, lo:hi, :] = jnp.zeros((2, hi - lo, H), F32)
    for lo in (0, 3 * H):
        ends_raw[:, :, lo : lo + H, :] = jnp.zeros((2, n // LANES, H, LANES), F32)

    my_row, my_col = offs_ref[0], offs_ref[1]
    weight = jnp.where(count_ref[0] > 0, 1.0, 0.0).astype(F32)
    for c in metas:
        c.arrived()
    above_row, above_col = jnp.max(near[0, 0]), jnp.max(near[0, 1])
    below_row, below_col = jnp.max(near[1, 0]), jnp.max(near[1, 1])
    left_row, right_row = jnp.max(near[2, 0]), jnp.max(near[3, 0])
    mate_row = jnp.where(even, below_row, above_row)
    mate_col = jnp.where(even, below_col, above_col)
    far_col = jnp.where(even, above_col, below_col)

    def take_columns(s, p, at, start):
        line = jnp.concatenate([hl[s, p, at, :], out[s, p, at, :], hr[s, p, at, :]], axis=1)
        return pltpu.roll(line, lax.rem(wide - start, wide), axis=1)[:, :n]

    def take_rows(field, part, start, height):
        strips = [field[part, q, pl.ds(start, height), :] for q in range(n // LANES)]
        return jnp.concatenate(strips, axis=1)

    def put_rows(field, part, rows, value):
        for q in range(n // LANES):
            field[part, q, rows, :] = value[:, q * LANES : (q + 1) * LANES]

    along = lambda chunks, source, target, there, here, device: [
        copies.remote(source.at[p, pl.ds(h, size)], target.at[p, pl.ds(h, size)], there, here, device)
        for p, h, size in chunks
    ]
    outers = [along(FORWARD[s], xs.at[s], xr.at[s], has_outward, has_inward, outward) for s in range(2)]
    inners = [along(FORWARD[s], ss.at[s], sr.at[s], always, always, partner) for s in range(2)]
    for s in range(2):
        loads[s][0].wait()
        if s:
            for c in halos[s][0]:
                c.arrived()
        for i, (p, h, size) in enumerate(FORWARD[s]):
            if not s and h == 0:
                for c in halo_first[p]:
                    c.arrived()
            at = pl.ds(pl.multiple_of(odd * last + h, SUBLANES), size)
            xs[s, p, pl.ds(h, size)] = take_columns(s, p, at, far_col)
            outers[s][i].start()
    for s in range(2):
        loads[s][1].wait()
        for c in halos[s][1]:
            c.arrived()
        for p in range(2):
            ss[s, p] = take_columns(s, p, mate_rows, mate_col)

    mate_near = jnp.where(even, mate_row <= half, mate_row > half)

    def pass_on(s, *which):
        for i in which:
            p, h, size = FORWARD[s][i]
            at = pl.ds(h, size)
            outers[s][i].arrived()
            ss[s, p, at] = jnp.where(mate_near, ss[s, p, at], xr[s, p, at])
            inners[s][i].start()

    for c in load_small[:3]:
        c.wait()

    def propagator(lo, hi):
        @pl.loop(lo // LANES, hi // LANES)
        def _(i):
            at = pl.ds(pl.multiple_of(i * LANES, LANES), LANES)
            phase = k[0, at, :]
            k[1, at, :] = jnp.sin(phase)
            k[0, at, :] = jnp.cos(phase)

    def fill_body(s, p):
        for lo in (0, last):
            put_rows(bodies[s], p, slice(H + lo, 2 * H + lo), take_columns(s, p, slice(lo, lo + H), my_col))

        @pl.loop(0, (last - H) // H)
        def _(i):
            at = pl.ds(pl.multiple_of(H + i * H, H), H)
            to = pl.ds(pl.multiple_of(2 * H + i * H, H), H)
            put_rows(bodies[s], p, to, take_columns(s, p, at, my_col))

    def body_ready(s):
        loads[s][2].wait()
        for c in halos[s][2]:
            c.arrived()

    make_tables(cos, sin, fwd, bwd)
    propagator(0, n // 2)
    pass_on(0, 0)
    propagator(n // 2, n)
    pass_on(0, 1)
    for c in load_small[3:]:
        c.wait()
    pass_on(0, 2)
    body_ready(0)
    fill_body(0, 0)
    pass_on(0, 3)
    fill_body(0, 1)
    pass_on(0, 4)

    def halo_rows(s):
        for c in inners[s]:
            c.arrived()
        for p in range(2):
            block = sr[s, p]
            put_rows(bodies[s], p, slice(0, H), block)
            put_rows(bodies[s], p, slice(tall - H, tall), block)

    window = lambda s, p, lo, height: take_rows(bodies[s], p, my_row + lo, height)
    full = lambda lo, height: (pl.ds(lo, height), pl.ds(n + lo, height))

    def stage_one(left, between=()):
        for i in range(2):
            mid[:, i * n : (i + 1) * n] = jnp.dot(
                left[i * n : (i + 1) * n, :], src[...], preferred_element_type=F32
            ).astype(BF16)
            for f in between[i : i + 1]:
                f()

    interior = ((H, n - H), (n + H, 2 * n - H))
    exterior = ((0, H), (n - H, n + H), (2 * n - H, 2 * n))

    def product(left, i, spans):
        rows = slice(i * n, (i + 1) * n)
        return jnp.dot(
            jnp.concatenate([left[rows, a:b] for a, b in spans], axis=1),
            jnp.concatenate([src[a:b, :] for a, b in spans], axis=0),
            preferred_element_type=F32,
        )

    def stage_two(right, spans, epilogue):
        rows = [mid[lo : lo + height, :] for lo, height in spans]
        rows = rows[0] if len(rows) == 1 else jnp.concatenate(rows, axis=0)
        result = jnp.dot(rows, right[...], preferred_element_type=F32)
        at = 0
        for lo, height in spans:
            epilogue(lo, height, result[at : at + height, :n], result[at : at + height, n:])
            at += height

    whole = [(0, n)]
    ends = [(0, H), (n - H, H)]
    middle = [(H, n - 2 * H)]

    def entry_wave(lo, height):
        at, low = full(lo, height)
        a_re = window(0, 0, lo, height)
        a_im = window(0, 1, lo, height)
        q_re, q_im = probe[0, at, :], probe[1, at, :]
        src[at, :] = (q_re * a_re - q_im * a_im).astype(BF16)
        src[low, :] = (q_re * a_im + q_im * a_re).astype(BF16)

    def first_product(wave, arrive):
        for lo in range(H, n - H, H):
            wave(lo, H)
        for i in range(2):
            share[i] = product(fwd, i, interior)
        arrive()
        for lo in (0, n - H):
            wave(lo, H)
        for i in range(2):
            mid[:, i * n : (i + 1) * n] = (share[i] + product(fwd, i, exterior)).astype(BF16)

    def first_halo():
        pass_on(1, 0)
        halo_rows(0)

    def second_halo():
        pass_on(1, 5)
        halo_rows(1)

    first_product(entry_wave, first_halo)

    def propagate(lo, height, re, im):
        at, low = full(lo, height)
        k_re, k_im = k[0, at, :], k[1, at, :]
        src[at, :] = (re * k_re - im * k_im).astype(BF16)
        src[low, :] = (re * k_im + im * k_re).astype(BF16)

    def keep(lo, height, re, im):
        at, _ = full(lo, height)
        psi[0, at, :] = re
        psi[1, at, :] = im

    def exit_wave(lo, height):
        at, low = full(lo, height)
        b_re = window(1, 0, lo, height)
        b_im = window(1, 1, lo, height)
        p_re, p_im = psi[0, at, :], psi[1, at, :]
        src[at, :] = (p_re * b_re - p_im * b_im).astype(BF16)
        src[low, :] = (p_re * b_im + p_im * b_re).astype(BF16)

    stage_two(bwd, whole, propagate)
    pass_on(1, 1)
    stage_one(bwd)
    body_ready(1)
    fill_body(1, 0)
    fill_body(1, 1)
    pass_on(1, 2)
    stage_two(fwd, whole, keep)
    pass_on(1, 3, 4)
    first_product(exit_wave, second_halo)

    def detect(lo, height, re, im):
        at, low = full(lo, height)
        factor = 1.0 - amp[at, :].astype(F32) / jnp.sqrt(re * re + im * im + 1.0)
        src[at, :] = (re * factor).astype(BF16)
        src[low, :] = (im * factor).astype(BF16)

    turn = lax.rem(my_col, LANES)

    def emit(s, p, lo, height, value):
        lane = lax.broadcasted_iota(jnp.int32, (height, LANES), 1)
        zero = jnp.zeros((height, LANES), F32)
        pieces = [value[:, q * LANES : (q + 1) * LANES] for q in range(n // LANES)]
        turned = [pltpu.roll(piece, turn, axis=1) for piece in pieces]
        at = pl.ds(first_row + lo, height)
        for q in range(tiles):
            before = turned[q - 1] if q else zero
            here = turned[q] if q < tiles - 1 else zero
            placed[p * tiles + q, at, :] = jnp.where(lane >= turn, here, before)
        own_l[s, p, pl.ds(lo, height), :] = jnp.where(lane >= my_col, turned[0], 0.0)
        own_r[s, p, pl.ds(lo, height), :] = jnp.where(lane < my_col - (inner + H - n), turned[-1], 0.0)
        if (lo, height) in ends:
            for q, piece in enumerate(pieces):
                ends_raw[p, q, pl.ds(H if lo == 0 else 2 * H, H), :] = piece

    def spread(lo, height, re, im):
        at, low = full(lo, height)
        p_re, p_im = psi[0, at, :], psi[1, at, :]
        b_re = window(1, 0, lo, height)
        b_im = window(1, 1, lo, height)
        emit(1, 0, lo, height, weight * (p_re * re + p_im * im))
        emit(1, 1, lo, height, weight * (p_re * im - p_im * re))
        src[at, :] = (b_re * re + b_im * im).astype(BF16)
        src[low, :] = (b_re * im - b_im * re).astype(BF16)

    spills = [along(BACKWARD[s], ss.at[s], orr.at[s], always, always, partner) for s in range(2)]
    relays = [along(BACKWARD[s], orr.at[s], ox.at[s], has_inward, has_outward, inward) for s in range(2)]
    early = [
        [
            to_left(own_l.at[s], grs[s].at[:, first_row : first_row + n, :]),
            to_right(own_r.at[s], gls[s].at[:, first_row : first_row + n, :]),
        ]
        for s in range(2)
    ]
    lates = [
        [
            [
                to_left(xs.at[s, p, pl.ds(h, size), : 2 * H], near_r.at[s, p, pl.ds(h, size)]),
                to_right(xs.at[s, p, pl.ds(h, size), 2 * H : 4 * H], near_l.at[s, p, pl.ds(h, size)]),
            ]
            for p, h, size in BACKWARD[s]
        ]
        for s in range(2)
    ]

    def spill(s):
        lower = tile_rows + 4 * H - n - jnp.maximum(my_row, tall - n - H)
        start = jnp.where(my_row <= half, H - jnp.minimum(my_row, H), lower)
        for c in inners[s]:
            c.sent()
        for i, (p, h, size) in enumerate(BACKWARD[s]):
            ss[s, p, pl.ds(h, size)] = take_rows(ends_raw, p, start + h, size)
            spills[s][i].start()

    def relay(s, *which):
        for i in which:
            spills[s][i].arrived()
            relays[s][i].start()

    def back(lo, height, re, im):
        at, low = full(lo, height)
        k_re, k_im = k[0, at, :], k[1, at, :]
        src[at, :] = (re * k_re + im * k_im).astype(BF16)
        src[low, :] = (im * k_re - re * k_im).astype(BF16)

    def finish(lo, height, re, im):
        at, _ = full(lo, height)
        q_re, q_im = probe[0, at, :], probe[1, at, :]
        emit(0, 0, lo, height, weight * (q_re * re + q_im * im))
        emit(0, 1, lo, height, weight * (q_re * im - q_im * re))

    spread_out = lambda block, start: pltpu.roll(
        jnp.concatenate([block, jnp.zeros((block.shape[0], wide - n), F32)], axis=1), start, axis=1
    )

    column = sum(jnp.where(my_col >= q * LANES, 1, 0) for q in range(1, (wide - n) // LANES + 1))

    def place_own(s, p):
        @pl.loop(0, tile_rows // H)
        def _(i):
            at = pl.ds(pl.multiple_of(i * H, H), H)
            for j in range(inner // LANES):
                tile = j + H // LANES - column
                inside = jnp.logical_and(tile >= 0, tile < tiles)
                tile = jnp.where(inside, p * tiles + tile, 2 * tiles)
                block = placed[tile, pl.ds(tall - n - my_row + i * H, H), :]
                lanes = slice(j * LANES, (j + 1) * LANES)
                out[s, p, at, lanes] -= step_ref[s] * block

    def place_near(s, i):
        p, h, size = BACKWARD[s][i]
        at = pl.ds(h, size)
        relays[s][i].arrived()
        for e, mine, start in (
            (0, jnp.logical_and(has_above, above_row > half), above_col),
            (1, jnp.logical_and(has_below, below_row <= half), below_col),
        ):
            outer = even if e == 0 else jnp.logical_not(even)
            block = jnp.where(outer, ox[s, p, at], orr[s, p, at])
            block = spread_out(jnp.where(mine, block, jnp.zeros_like(block)), start)
            xs[s, p, at, e * H : (e + 1) * H] = block[:, :H]
            xs[s, p, at, (2 + e) * H : (3 + e) * H] = block[:, H + inner :]
            rows = pl.ds(e * last + h, size)
            out[s, p, rows, :] -= step_ref[s] * block[:, H : H + inner]
        for c in lates[s][i]:
            c.start()

    def sides(s):
        for c in early[s]:
            c.arrived()
        for p in range(2):

            @pl.loop(0, tile_rows // H)
            def _(i, p=p):
                at = pl.ds(pl.multiple_of(i * H, H), H)
                from_left = gls[s][p, pl.ds(tall - n - left_row + i * H, H), :]
                from_right = grs[s][p, pl.ds(tall - n - right_row + i * H, H), :]
                out[s, p, at, :H] -= step_ref[s] * from_left
                out[s, p, at, inner - H :] -= step_ref[s] * from_right

    def corners(s, i):
        p, h, size = BACKWARD[s][i]
        for c in lates[s][i]:
            c.arrived()
        for e in range(2):
            at = pl.ds(e * last + h, size)
            out[s, p, at, :H] -= step_ref[s] * near_l[s, p, pl.ds(h, size), e * H : (e + 1) * H]
            out[s, p, at, inner - H :] -= step_ref[s] * near_r[s, p, pl.ds(h, size), e * H : (e + 1) * H]

    stage_two(bwd, whole, detect)
    stage_one(bwd)
    stage_two(fwd, ends, spread)
    spill(1)
    stage_two(fwd, middle, spread)
    for c in early[1]:
        c.start()
    stage_one(fwd)
    stage_two(bwd, whole, back)
    place_own(1, 0)
    place_own(1, 1)
    relay(1, 0)
    stage_one(bwd)
    stage_two(fwd, ends, finish)
    spill(0)
    relay(1, 1)
    stage_two(fwd, middle, finish)
    for c in early[0]:
        c.start()
    for c in outers[0] + outers[1]:
        c.sent()
    place_own(0, 0)
    place_own(0, 1)
    relay(1, 2)
    place_near(1, 0)
    relay(1, 3)
    place_near(1, 1)
    sides(1)
    relay(0, 0)
    place_near(1, 2)
    place_near(1, 3)
    relay(0, 1)
    sides(0)
    relay(0, 2)
    for i in range(4):
        corners(1, i)
    place_near(0, 0)
    relay(0, 3, 4, 5)
    for i in range(1, 6):
        place_near(0, i)
    for i in range(6):
        corners(0, i)

    for c in copies.remotes:
        if not c.waited:
            c.sent()
    assert len(copies.remotes) == REMOTES and copies.local_used == LOCALS


def write_kernel(done, out, sems):
    copies = []
    rows = done.shape[2] // 3
    for i in range(12):
        at = (i // 6, i // 3 % 2, pl.ds(i % 3 * rows, rows))
        copies.append(pltpu.make_async_copy(done.at[at], out.at[at], sems.at[i]))
    for c in copies:
        c.start()
    for c in copies:
        c.wait()


def per_device(object_tiles, probe, prop_phase, amplitudes, offsets, counts, step_size):
    n = probe.shape[1]
    rows, inner = object_tiles.shape[2:]
    cos, sin = dft_table(n)
    tall = rows + 2 * H
    smem = pl.BlockSpec(memory_space=pltpu.SMEM)
    anywhere = pl.BlockSpec(memory_space=pl.ANY)
    on_chip = pl.BlockSpec(memory_space=pltpu.VMEM)
    vmem = lambda *shape, kind=F32: pltpu.VMEM(shape, kind)
    block = vmem(2, 2, H, n)
    long = 2 * tall - n - 2 * H
    scratch = (
        [vmem(2, SUBLANES, LANES, kind=jnp.int32), vmem(4, 2, SUBLANES, LANES, kind=jnp.int32)]
        + [vmem(2, n, n), vmem(2, n, n)]
        + [vmem(n, n, kind=BF16)] * 3
        + [vmem(2 * n, 2 * n, kind=BF16)] * 2
        + [vmem(2 * n, n, kind=BF16), vmem(n, 2 * n, kind=BF16), vmem(2, n, n)]
        + [vmem(2, 2, rows, H)] * 2
        + [vmem(2, n // LANES, tall, LANES)] * 2
        + [block] * 4
        + [vmem(2 * (n // LANES + 1) + 1, long, LANES), vmem(2, n // LANES, 4 * H, LANES), vmem(2, n, n)]
        + [block] * 2
        + [vmem(2, 2, n, H)] * 2
        + [vmem(2, long, H)] * 4
        + [vmem(2, 2, H, 2 * H)] * 2
        + [pltpu.SemaphoreType.DMA((REMOTES,))] * 2
        + [pltpu.SemaphoreType.DMA((LOCALS,))]
    )
    done = pl.pallas_call(
        step_kernel,
        in_specs=[smem] * 3 + [anywhere] * 6,
        out_specs=on_chip,
        out_shape=pltpu.VMEM(object_tiles.shape, F32),
        scratch_shapes=scratch,
        name="step",
        compiler_params=pltpu.CompilerParams(
            collective_id=0, has_side_effects=True, vmem_limit_bytes=VMEM_LIMIT
        ),
    )(offsets[0, 0, 0], counts[0], step_size, object_tiles, probe, prop_phase, amplitudes, cos, sin)
    return pl.pallas_call(
        write_kernel,
        in_specs=[on_chip],
        out_specs=anywhere,
        out_shape=jax.ShapeDtypeStruct(object_tiles.shape, F32),
        scratch_shapes=[pltpu.SemaphoreType.DMA((12,))],
        name="write",
        compiler_params=pltpu.CompilerParams(vmem_limit_bytes=1 << 20),
    )(done)


VMEM_LIMIT = 54 << 20


def solution(mesh):
    return jax.shard_map(
        per_device,
        mesh=mesh,
        in_specs=(
            P(None, None, "rows", "cols"),
            P(),
            P(),
            P("rows", "cols", None, None, None),
            P("rows", "cols", None, None),
            P("rows", "cols"),
            P(),
        ),
        out_specs=P(None, None, "rows", "cols"),
        check_vma=False,
    )
```

```python
import math

import jax
import jax.numpy as jnp
import numpy as np
from jax import lax
from jax.experimental import pallas as pl
from jax.experimental.pallas import tpu as pltpu
from jax.sharding import PartitionSpec as P

H = 128
LANES = 128
SUBLANES = 8
EVEN_CHUNKS = [(p, h, H // 2) for p in range(2) for h in (0, H // 2)]
FIRST_SMALL = [(0, 0, H // 4), (0, H // 4, H // 4)] + EVEN_CHUNKS[1:]
LAST_SMALL = EVEN_CHUNKS[:3] + [(1, H // 2, H // 4), (1, 3 * H // 4, H // 4)]
FORWARD = (FIRST_SMALL, EVEN_CHUNKS)
BACKWARD = (LAST_SMALL, EVEN_CHUNKS)
F32 = jnp.float32
BF16 = jnp.bfloat16
MESH = pl.DeviceIdType.MESH


def dft_table(length):
    index = np.arange(length, dtype=np.int64)
    angles = ((index[:, None] * index[None, :]) % length).astype(np.float32) * np.float32(
        2.0 * math.pi / length
    )
    scaling = np.float32(1.0 / math.sqrt(length))
    return (
        jnp.asarray((np.cos(angles) * scaling).astype(BF16)),
        jnp.asarray((-np.sin(angles) * scaling).astype(BF16)),
    )


def make_tables(cos_ref, sin_ref, fwd, bwd):
    n = cos_ref.shape[0]
    c, s = cos_ref[...], sin_ref[...]
    for table, sine in ((fwd, s), (bwd, -s)):
        table[:n, :n] = c
        table[n:, n:] = c
        table[n:, :n] = sine
        table[:n, n:] = -sine


class Copies:
    def __init__(self, sends, receives, locals_):
        self.sends, self.receives, self.locals = sends, receives, locals_
        self.remotes = []
        self.local_used = 0

    def remote(self, src, dst, there, here, device):
        k = len(self.remotes)
        copy = pltpu.make_async_remote_copy(
            src_ref=src,
            dst_ref=dst,
            send_sem=self.sends.at[k],
            recv_sem=self.receives.at[k],
            device_id=device,
            device_id_type=MESH,
        )
        self.remotes.append(Remote(copy, there, here))
        return self.remotes[-1]

    def local(self, src, dst):
        k = self.local_used
        self.local_used += 1
        return pltpu.make_async_copy(src, dst, self.locals.at[k])


class Remote:
    def __init__(self, copy, there, here):
        self.copy, self.there, self.here = copy, there, here
        self.waited = False

    def start(self):
        pl.when(self.there)(lambda: self.copy.start())

    def arrived(self):
        pl.when(self.here)(lambda: self.copy.wait_recv())

    def sent(self):
        self.waited = True
        pl.when(self.there)(lambda: self.copy.wait_send())


REMOTES = 22 + 2 * sum(map(len, FORWARD)) + 4 * sum(map(len, BACKWARD))
LOCALS = 5 + 2 * 3


def step_kernel(
    offs_ref, count_ref, step_ref, obj, probe_in, phase_in, amp_in, cos_in, sin_in, out,
    meta, near, probe, k, amp, cos, sin, fwd, bwd, src, mid, psi,
    hl, hr, body0, body1, xs, xr, ss, sr, placed, ends_raw, share,
    orr, ox, own_l, own_r, gl0, gl1, gr0, gr1, near_l, near_r,
    sends, receives, locals_,
):
    n = cos.shape[0]
    tile_rows, inner = obj.shape[2:]
    wide = inner + 2 * H
    tall = tile_rows + 2 * H
    half = (tall - n) // 2
    last = tile_rows - H
    bodies, gls, grs = (body0, body1), (gl0, gl1), (gr0, gr1)

    me_r, me_c = lax.axis_index("rows"), lax.axis_index("cols")
    n_r, n_c = lax.axis_size("rows"), lax.axis_size("cols")
    odd = lax.rem(me_r, 2)
    even = odd == 0
    side = 1 - 2 * odd
    has_left, has_right = me_c > 0, me_c < n_c - 1
    has_above, has_below = me_r > 0, me_r < n_r - 1
    far_above, far_below = me_r > 1, me_r < n_r - 2
    row = lambda r: {"rows": r, "cols": me_c}
    col = lambda c: {"rows": me_r, "cols": c}
    partner = row(me_r + side)
    outward = row(me_r - 2 * side)
    inward = row(me_r + 2 * side)
    has_outward = jnp.where(even, me_r - 2, n_r - 3 - me_r) >= 0
    has_inward = jnp.where(even, n_r - 3 - me_r, me_r - 2) >= 0
    always = me_r >= 0

    copies = Copies(sends, receives, locals_)
    far_rows = pl.ds(pl.multiple_of(odd * last, H), H)
    mate_rows = pl.ds(pl.multiple_of((1 - odd) * last, H), H)
    mid_rows = pl.ds(H, last - H)
    pieces = (far_rows, mate_rows, mid_rows)

    loads = [[copies.local(obj.at[s, :, at, :], out.at[s, :, at, :]) for at in pieces] for s in range(2)]
    load_small = [
        copies.local(a, b)
        for a, b in ((cos_in, cos), (sin_in, sin), (phase_in, k.at[0]), (probe_in, probe), (amp_in.at[0, 0, 0], amp))
    ]
    for c in loads[0][:2] + loads[1][:2] + load_small[:3] + loads[0][2:] + load_small[3:] + loads[1][2:]:
        c.start()
    for i in range(2):
        meta[i] = jnp.full(meta.shape[1:], offs_ref[i], jnp.int32)

    barrier = pltpu.get_barrier_semaphore()
    greeted = (
        (has_left, col(me_c - 1)), (has_right, col(me_c + 1)),
        (has_above, row(me_r - 1)), (has_below, row(me_r + 1)),
        (far_above, row(me_r - 2)), (far_below, row(me_r + 2)),
    )
    total = jnp.int32(0)
    for exists, device in greeted:
        total += exists.astype(jnp.int32)

        @pl.when(exists)
        def _(device=device):
            pl.semaphore_signal(barrier, inc=1, device_id=device, device_id_type=MESH)

    first_row = tall - n - H

    @pl.when(jnp.logical_not(has_left))
    def _():
        hl[...] = jnp.zeros_like(hl)
        near_l[...] = jnp.zeros_like(near_l)
        for ref in gls:
            ref[:, first_row : first_row + n, :] = jnp.zeros((2, n, H), F32)

    @pl.when(jnp.logical_not(has_right))
    def _():
        hr[...] = jnp.zeros_like(hr)
        near_r[...] = jnp.zeros_like(near_r)
        for ref in grs:
            ref[:, first_row : first_row + n, :] = jnp.zeros((2, n, H), F32)

    @pl.when(jnp.logical_not(has_inward))
    def _():
        xr[...] = jnp.zeros_like(xr)

    @pl.when(jnp.logical_not(has_outward))
    def _():
        ox[...] = jnp.zeros_like(ox)

    for i, exists in enumerate((has_above, has_below, has_left, has_right)):

        @pl.when(jnp.logical_not(exists))
        def _(i=i):
            near[i] = jnp.zeros(near.shape[1:], jnp.int32)

    pl.semaphore_wait(barrier, total)

    to_right = lambda a, b: copies.remote(a, b, has_right, has_left, col(me_c + 1))
    to_left = lambda a, b: copies.remote(a, b, has_left, has_right, col(me_c - 1))
    metas = [
        copies.remote(meta, near.at[0], has_below, has_above, row(me_r + 1)),
        copies.remote(meta, near.at[1], has_above, has_below, row(me_r - 1)),
        to_right(meta, near.at[2]),
        to_left(meta, near.at[3]),
    ]
    def halo(s, at, p=slice(None)):
        return [
            to_right(obj.at[s, p, at, inner - H :], hl.at[s, p, at, :]),
            to_left(obj.at[s, p, at, 0:H], hr.at[s, p, at, :]),
        ]

    halos = [[halo(s, at) for at in pieces] if s else [None] + [halo(s, at) for at in pieces[1:]] for s in range(2)]
    halo_first = [halo(0, far_rows, p) for p in range(2)]
    halos[0][0] = halo_first[0] + halo_first[1]
    for group in (metas, halos[0][0], halos[0][1], halos[1][0], halos[1][1], halos[0][2], halos[1][2]):
        for c in group:
            c.start()

    tiles = n // LANES + 1
    long = placed.shape[1]

    @pl.loop(0, 2 * tiles)
    def _(q):
        placed[q, :first_row, :] = jnp.zeros((first_row, LANES), F32)
        placed[q, first_row + n :, :] = jnp.zeros((first_row, LANES), F32)

    placed[2 * tiles] = jnp.zeros((long, LANES), F32)
    for lo, hi in ((0, first_row), (first_row + n, long)):
        for ref in gls + grs:
            ref[:, lo:hi, :] = jnp.zeros((2, hi - lo, H), F32)
    for lo in (0, 3 * H):
        ends_raw[:, :, lo : lo + H, :] = jnp.zeros((2, n // LANES, H, LANES), F32)

    my_row, my_col = offs_ref[0], offs_ref[1]
    weight = jnp.where(count_ref[0] > 0, 1.0, 0.0).astype(F32)
    for c in metas:
        c.arrived()
    above_row, above_col = jnp.max(near[0, 0]), jnp.max(near[0, 1])
    below_row, below_col = jnp.max(near[1, 0]), jnp.max(near[1, 1])
    left_row, right_row = jnp.max(near[2, 0]), jnp.max(near[3, 0])
    mate_row = jnp.where(even, below_row, above_row)
    mate_col = jnp.where(even, below_col, above_col)
    far_col = jnp.where(even, above_col, below_col)

    def take_columns(s, p, at, start):
        line = jnp.concatenate([hl[s, p, at, :], out[s, p, at, :], hr[s, p, at, :]], axis=1)
        return pltpu.roll(line, lax.rem(wide - start, wide), axis=1)[:, :n]

    def take_rows(field, part, start, height):
        strips = [field[part, q, pl.ds(start, height), :] for q in range(n // LANES)]
        return jnp.concatenate(strips, axis=1)

    def put_rows(field, part, rows, value):
        for q in range(n // LANES):
            field[part, q, rows, :] = value[:, q * LANES : (q + 1) * LANES]

    along = lambda chunks, source, target, there, here, device: [
        copies.remote(source.at[p, pl.ds(h, size)], target.at[p, pl.ds(h, size)], there, here, device)
        for p, h, size in chunks
    ]
    outers = [along(FORWARD[s], xs.at[s], xr.at[s], has_outward, has_inward, outward) for s in range(2)]
    inners = [along(FORWARD[s], ss.at[s], sr.at[s], always, always, partner) for s in range(2)]
    def send_far(s):
        loads[s][0].wait()
        if s:
            for c in halos[s][0]:
                c.arrived()
        for i, (p, h, size) in enumerate(FORWARD[s]):
            if not s and h == 0:
                for c in halo_first[p]:
                    c.arrived()
            at = pl.ds(pl.multiple_of(odd * last + h, SUBLANES), size)
            xs[s, p, pl.ds(h, size)] = take_columns(s, p, at, far_col)
            outers[s][i].start()

    def take_mate(s):
        loads[s][1].wait()
        for c in halos[s][1]:
            c.arrived()
        for p in range(2):
            ss[s, p] = take_columns(s, p, mate_rows, mate_col)

    send_far(0)
    take_mate(0)
    mate_near = jnp.where(even, mate_row <= half, mate_row > half)

    def pass_on(s, *which):
        for i in which:
            p, h, size = FORWARD[s][i]
            at = pl.ds(h, size)
            outers[s][i].arrived()
            ss[s, p, at] = jnp.where(mate_near, ss[s, p, at], xr[s, p, at])
            inners[s][i].start()

    def propagator(lo, hi):
        @pl.loop(lo // LANES, hi // LANES)
        def _(i):
            at = pl.ds(pl.multiple_of(i * LANES, LANES), LANES)
            phase = k[0, at, :]
            k[1, at, :] = jnp.sin(phase)
            k[0, at, :] = jnp.cos(phase)

    def fill_body(s, p):
        for lo in (0, last):
            put_rows(bodies[s], p, slice(H + lo, 2 * H + lo), take_columns(s, p, slice(lo, lo + H), my_col))

        @pl.loop(0, (last - H) // H)
        def _(i):
            at = pl.ds(pl.multiple_of(H + i * H, H), H)
            to = pl.ds(pl.multiple_of(2 * H + i * H, H), H)
            put_rows(bodies[s], p, to, take_columns(s, p, at, my_col))

    def body_ready(s):
        loads[s][2].wait()
        for c in halos[s][2]:
            c.arrived()

    pass_on(0, 0)
    send_far(1)
    pass_on(0, 1)
    take_mate(1)
    pass_on(0, 2)
    for c in load_small:
        c.wait()
    make_tables(cos, sin, fwd, bwd)
    propagator(0, n // 2)
    pass_on(0, 3)
    propagator(n // 2, n)
    pass_on(0, 4)
    body_ready(0)
    fill_body(0, 0)
    fill_body(0, 1)

    def halo_rows(s):
        for c in inners[s]:
            c.arrived()
        for p in range(2):
            block = sr[s, p]
            put_rows(bodies[s], p, slice(0, H), block)
            put_rows(bodies[s], p, slice(tall - H, tall), block)

    window = lambda s, p, lo, height: take_rows(bodies[s], p, my_row + lo, height)
    full = lambda lo, height: (pl.ds(lo, height), pl.ds(n + lo, height))

    def stage_one(left, between=()):
        for i in range(2):
            mid[:, i * n : (i + 1) * n] = jnp.dot(
                left[i * n : (i + 1) * n, :], src[...], preferred_element_type=F32
            ).astype(BF16)
            for f in between[i : i + 1]:
                f()

    interior = ((H, n - H), (n + H, 2 * n - H))
    exterior = ((0, H), (n - H, n + H), (2 * n - H, 2 * n))

    def product(left, i, spans):
        rows = slice(i * n, (i + 1) * n)
        return jnp.dot(
            jnp.concatenate([left[rows, a:b] for a, b in spans], axis=1),
            jnp.concatenate([src[a:b, :] for a, b in spans], axis=0),
            preferred_element_type=F32,
        )

    def stage_two(right, spans, epilogue):
        rows = [mid[lo : lo + height, :] for lo, height in spans]
        rows = rows[0] if len(rows) == 1 else jnp.concatenate(rows, axis=0)
        result = jnp.dot(rows, right[...], preferred_element_type=F32)
        at = 0
        for lo, height in spans:
            epilogue(lo, height, result[at : at + height, :n], result[at : at + height, n:])
            at += height

    whole = [(0, n)]
    ends = [(0, H), (n - H, H)]
    middle = [(H, n - 2 * H)]

    halo_rows(0)
    pass_on(1, 0)

    @pl.loop(0, n // H)
    def _(i):
        at = pl.ds(pl.multiple_of(i * H, H), H)
        low = pl.ds(pl.multiple_of(n + i * H, H), H)
        a_re = window(0, 0, i * H, H)
        a_im = window(0, 1, i * H, H)
        q_re, q_im = probe[0, at, :], probe[1, at, :]
        src[at, :] = (q_re * a_re - q_im * a_im).astype(BF16)
        src[low, :] = (q_re * a_im + q_im * a_re).astype(BF16)

    def propagate(lo, height, re, im):
        at, low = full(lo, height)
        k_re, k_im = k[0, at, :], k[1, at, :]
        src[at, :] = (re * k_re - im * k_im).astype(BF16)
        src[low, :] = (re * k_im + im * k_re).astype(BF16)

    def keep(lo, height, re, im):
        at, _ = full(lo, height)
        psi[0, at, :] = re
        psi[1, at, :] = im

    def exit_wave(lo, height):
        at, low = full(lo, height)
        b_re = window(1, 0, lo, height)
        b_im = window(1, 1, lo, height)
        p_re, p_im = psi[0, at, :], psi[1, at, :]
        src[at, :] = (p_re * b_re - p_im * b_im).astype(BF16)
        src[low, :] = (p_re * b_im + p_im * b_re).astype(BF16)

    stage_one(fwd)
    stage_two(bwd, whole, propagate)
    pass_on(1, 1)
    stage_one(bwd)
    body_ready(1)
    fill_body(1, 0)
    pass_on(1, 2)
    stage_two(fwd, whole, keep)
    pass_on(1, 3)
    fill_body(1, 1)
    for lo in range(H, n - H, H):
        exit_wave(lo, H)
    for i in range(2):
        share[i] = product(fwd, i, interior)
    halo_rows(1)
    for lo in (0, n - H):
        exit_wave(lo, H)

    def detect(lo, height, re, im):
        at, low = full(lo, height)
        factor = 1.0 - amp[at, :].astype(F32) / jnp.sqrt(re * re + im * im + 1.0)
        src[at, :] = (re * factor).astype(BF16)
        src[low, :] = (im * factor).astype(BF16)

    turn = lax.rem(my_col, LANES)

    def emit(s, p, lo, height, value):
        lane = lax.broadcasted_iota(jnp.int32, (height, LANES), 1)
        zero = jnp.zeros((height, LANES), F32)
        pieces = [value[:, q * LANES : (q + 1) * LANES] for q in range(n // LANES)]
        turned = [pltpu.roll(piece, turn, axis=1) for piece in pieces]
        at = pl.ds(first_row + lo, height)
        for q in range(tiles):
            before = turned[q - 1] if q else zero
            here = turned[q] if q < tiles - 1 else zero
            placed[p * tiles + q, at, :] = jnp.where(lane >= turn, here, before)
        own_l[s, p, pl.ds(lo, height), :] = jnp.where(lane >= my_col, turned[0], 0.0)
        own_r[s, p, pl.ds(lo, height), :] = jnp.where(lane < my_col - (inner + H - n), turned[-1], 0.0)
        if (lo, height) in ends:
            for q, piece in enumerate(pieces):
                ends_raw[p, q, pl.ds(H if lo == 0 else 2 * H, H), :] = piece

    def spread(lo, height, re, im):
        at, low = full(lo, height)
        p_re, p_im = psi[0, at, :], psi[1, at, :]
        b_re = window(1, 0, lo, height)
        b_im = window(1, 1, lo, height)
        emit(1, 0, lo, height, weight * (p_re * re + p_im * im))
        emit(1, 1, lo, height, weight * (p_re * im - p_im * re))
        src[at, :] = (b_re * re + b_im * im).astype(BF16)
        src[low, :] = (b_re * im - b_im * re).astype(BF16)

    spills = [along(BACKWARD[s], ss.at[s], orr.at[s], always, always, partner) for s in range(2)]
    relays = [along(BACKWARD[s], orr.at[s], ox.at[s], has_inward, has_outward, inward) for s in range(2)]
    early = [
        [
            to_left(own_l.at[s], grs[s].at[:, first_row : first_row + n, :]),
            to_right(own_r.at[s], gls[s].at[:, first_row : first_row + n, :]),
        ]
        for s in range(2)
    ]
    lates = [
        [
            [
                to_left(xs.at[s, p, pl.ds(h, size), : 2 * H], near_r.at[s, p, pl.ds(h, size)]),
                to_right(xs.at[s, p, pl.ds(h, size), 2 * H : 4 * H], near_l.at[s, p, pl.ds(h, size)]),
            ]
            for p, h, size in BACKWARD[s]
        ]
        for s in range(2)
    ]

    def spill(s):
        lower = tile_rows + 4 * H - n - jnp.maximum(my_row, tall - n - H)
        start = jnp.where(my_row <= half, H - jnp.minimum(my_row, H), lower)
        for c in inners[s]:
            c.sent()
        for i, (p, h, size) in enumerate(BACKWARD[s]):
            ss[s, p, pl.ds(h, size)] = take_rows(ends_raw, p, start + h, size)
            spills[s][i].start()

    def relay(s, *which):
        for i in which:
            spills[s][i].arrived()
            relays[s][i].start()

    def back(lo, height, re, im):
        at, low = full(lo, height)
        k_re, k_im = k[0, at, :], k[1, at, :]
        src[at, :] = (re * k_re + im * k_im).astype(BF16)
        src[low, :] = (im * k_re - re * k_im).astype(BF16)

    def finish(lo, height, re, im):
        at, _ = full(lo, height)
        q_re, q_im = probe[0, at, :], probe[1, at, :]
        emit(0, 0, lo, height, weight * (q_re * re + q_im * im))
        emit(0, 1, lo, height, weight * (q_re * im - q_im * re))

    spread_out = lambda block, start: pltpu.roll(
        jnp.concatenate([block, jnp.zeros((block.shape[0], wide - n), F32)], axis=1), start, axis=1
    )

    column = sum(jnp.where(my_col >= q * LANES, 1, 0) for q in range(1, (wide - n) // LANES + 1))

    def place_own(s, p):
        @pl.loop(0, tile_rows // H)
        def _(i):
            at = pl.ds(pl.multiple_of(i * H, H), H)
            for j in range(inner // LANES):
                tile = j + H // LANES - column
                inside = jnp.logical_and(tile >= 0, tile < tiles)
                tile = jnp.where(inside, p * tiles + tile, 2 * tiles)
                block = placed[tile, pl.ds(tall - n - my_row + i * H, H), :]
                lanes = slice(j * LANES, (j + 1) * LANES)
                out[s, p, at, lanes] -= step_ref[s] * block

    def place_near(s, i):
        p, h, size = BACKWARD[s][i]
        at = pl.ds(h, size)
        relays[s][i].arrived()
        for e, mine, start in (
            (0, jnp.logical_and(has_above, above_row > half), above_col),
            (1, jnp.logical_and(has_below, below_row <= half), below_col),
        ):
            outer = even if e == 0 else jnp.logical_not(even)
            block = jnp.where(outer, ox[s, p, at], orr[s, p, at])
            block = spread_out(jnp.where(mine, block, jnp.zeros_like(block)), start)
            xs[s, p, at, e * H : (e + 1) * H] = block[:, :H]
            xs[s, p, at, (2 + e) * H : (3 + e) * H] = block[:, H + inner :]
            rows = pl.ds(e * last + h, size)
            out[s, p, rows, :] -= step_ref[s] * block[:, H : H + inner]
        for c in lates[s][i]:
            c.start()

    def sides(s):
        for c in early[s]:
            c.arrived()
        for p in range(2):

            @pl.loop(0, tile_rows // H)
            def _(i, p=p):
                at = pl.ds(pl.multiple_of(i * H, H), H)
                from_left = gls[s][p, pl.ds(tall - n - left_row + i * H, H), :]
                from_right = grs[s][p, pl.ds(tall - n - right_row + i * H, H), :]
                out[s, p, at, :H] -= step_ref[s] * from_left
                out[s, p, at, inner - H :] -= step_ref[s] * from_right

    def corners(s, i):
        p, h, size = BACKWARD[s][i]
        for c in lates[s][i]:
            c.arrived()
        for e in range(2):
            at = pl.ds(e * last + h, size)
            out[s, p, at, :H] -= step_ref[s] * near_l[s, p, pl.ds(h, size), e * H : (e + 1) * H]
            out[s, p, at, inner - H :] -= step_ref[s] * near_r[s, p, pl.ds(h, size), e * H : (e + 1) * H]

    for i in range(2):
        mid[:, i * n : (i + 1) * n] = (share[i] + product(fwd, i, exterior)).astype(BF16)
    stage_two(bwd, whole, detect)
    stage_one(bwd)
    stage_two(fwd, ends, spread)
    spill(1)
    stage_two(fwd, middle, spread)
    for c in early[1]:
        c.start()
    stage_one(fwd)
    relay(1, 0)
    stage_two(bwd, whole, back)
    place_own(1, 0)
    relay(1, 1)
    place_own(1, 1)
    stage_one(bwd)
    stage_two(fwd, ends, finish)
    spill(0)
    relay(1, 2)
    stage_two(fwd, middle, finish)
    for c in early[0]:
        c.start()
    for c in outers[0] + outers[1]:
        c.sent()
    relay(1, 3)
    place_near(1, 0)
    place_near(1, 1)
    place_own(0, 0)
    relay(0, 0)
    place_near(1, 2)
    place_near(1, 3)
    place_own(0, 1)
    relay(0, 1)
    sides(1)
    relay(0, 2)
    for i in range(4):
        corners(1, i)
    place_near(0, 0)
    relay(0, 3)
    place_near(0, 1)
    relay(0, 4)
    sides(0)
    for i in range(2, 5):
        place_near(0, i)
    for i in range(5):
        corners(0, i)

    for c in copies.remotes:
        if not c.waited:
            c.sent()
    assert len(copies.remotes) == REMOTES and copies.local_used == LOCALS


def write_kernel(done, out, sems):
    copies = []
    rows = done.shape[2] // 3
    for i in range(12):
        at = (i // 6, i // 3 % 2, pl.ds(i % 3 * rows, rows))
        copies.append(pltpu.make_async_copy(done.at[at], out.at[at], sems.at[i]))
    for c in copies:
        c.start()
    for c in copies:
        c.wait()


def per_device(object_tiles, probe, prop_phase, amplitudes, offsets, counts, step_size):
    n = probe.shape[1]
    rows, inner = object_tiles.shape[2:]
    cos, sin = dft_table(n)
    tall = rows + 2 * H
    smem = pl.BlockSpec(memory_space=pltpu.SMEM)
    anywhere = pl.BlockSpec(memory_space=pl.ANY)
    on_chip = pl.BlockSpec(memory_space=pltpu.VMEM)
    vmem = lambda *shape, kind=F32: pltpu.VMEM(shape, kind)
    block = vmem(2, 2, H, n)
    long = 2 * tall - n - 2 * H
    scratch = (
        [vmem(2, SUBLANES, LANES, kind=jnp.int32), vmem(4, 2, SUBLANES, LANES, kind=jnp.int32)]
        + [vmem(2, n, n), vmem(2, n, n)]
        + [vmem(n, n, kind=BF16)] * 3
        + [vmem(2 * n, 2 * n, kind=BF16)] * 2
        + [vmem(2 * n, n, kind=BF16), vmem(n, 2 * n, kind=BF16), vmem(2, n, n)]
        + [vmem(2, 2, rows, H)] * 2
        + [vmem(2, n // LANES, tall, LANES)] * 2
        + [block] * 4
        + [vmem(2 * (n // LANES + 1) + 1, long, LANES), vmem(2, n // LANES, 4 * H, LANES), vmem(2, n, n)]
        + [block] * 2
        + [vmem(2, 2, n, H)] * 2
        + [vmem(2, long, H)] * 4
        + [vmem(2, 2, H, 2 * H)] * 2
        + [pltpu.SemaphoreType.DMA((REMOTES,))] * 2
        + [pltpu.SemaphoreType.DMA((LOCALS,))]
    )
    done = pl.pallas_call(
        step_kernel,
        in_specs=[smem] * 3 + [anywhere] * 6,
        out_specs=on_chip,
        out_shape=pltpu.VMEM(object_tiles.shape, F32),
        scratch_shapes=scratch,
        name="step",
        compiler_params=pltpu.CompilerParams(
            collective_id=0, has_side_effects=True, vmem_limit_bytes=VMEM_LIMIT
        ),
    )(offsets[0, 0, 0], counts[0], step_size, object_tiles, probe, prop_phase, amplitudes, cos, sin)
    return pl.pallas_call(
        write_kernel,
        in_specs=[on_chip],
        out_specs=anywhere,
        out_shape=jax.ShapeDtypeStruct(object_tiles.shape, F32),
        scratch_shapes=[pltpu.SemaphoreType.DMA((12,))],
        name="write",
        compiler_params=pltpu.CompilerParams(vmem_limit_bytes=1 << 20),
    )(done)


VMEM_LIMIT = 54 << 20


def solution(mesh):
    return jax.shard_map(
        per_device,
        mesh=mesh,
        in_specs=(
            P(None, None, "rows", "cols"),
            P(),
            P(),
            P("rows", "cols", None, None, None),
            P("rows", "cols", None, None),
            P("rows", "cols"),
            P(),
        ),
        out_specs=P(None, None, "rows", "cols"),
        check_vma=False,
    )
```

```python
import math

import jax
import jax.numpy as jnp
import numpy as np
from jax import lax
from jax.experimental import pallas as pl
from jax.experimental.pallas import tpu as pltpu
from jax.sharding import PartitionSpec as P

H = 128
LANES = 128
SUBLANES = 8
EVEN_CHUNKS = [(p, h, H // 2) for p in range(2) for h in (0, H // 2)]
FIRST_SMALL = [(0, 0, H // 4), (0, H // 4, H // 4)] + EVEN_CHUNKS[1:]
LAST_SMALL = EVEN_CHUNKS[:3] + [(1, H // 2, H // 4), (1, 3 * H // 4, H // 4)]
FORWARD = (FIRST_SMALL, EVEN_CHUNKS)
BACKWARD = (LAST_SMALL, EVEN_CHUNKS)
F32 = jnp.float32
BF16 = jnp.bfloat16
MESH = pl.DeviceIdType.MESH


def dft_table(length):
    index = np.arange(length, dtype=np.int64)
    angles = ((index[:, None] * index[None, :]) % length).astype(np.float32) * np.float32(
        2.0 * math.pi / length
    )
    scaling = np.float32(1.0 / math.sqrt(length))
    return (
        jnp.asarray((np.cos(angles) * scaling).astype(BF16)),
        jnp.asarray((-np.sin(angles) * scaling).astype(BF16)),
    )


def make_tables(cos_ref, sin_ref, fwd, bwd):
    n = cos_ref.shape[0]
    c, s = cos_ref[...], sin_ref[...]
    for table, sine in ((fwd, s), (bwd, -s)):
        table[:n, :n] = c
        table[n:, n:] = c
        table[n:, :n] = sine
        table[:n, n:] = -sine


class Copies:
    def __init__(self, sends, receives, locals_):
        self.sends, self.receives, self.locals = sends, receives, locals_
        self.remotes = []
        self.local_used = 0

    def remote(self, src, dst, there, here, device):
        k = len(self.remotes)
        copy = pltpu.make_async_remote_copy(
            src_ref=src,
            dst_ref=dst,
            send_sem=self.sends.at[k],
            recv_sem=self.receives.at[k],
            device_id=device,
            device_id_type=MESH,
        )
        self.remotes.append(Remote(copy, there, here))
        return self.remotes[-1]

    def local(self, src, dst):
        k = self.local_used
        self.local_used += 1
        return pltpu.make_async_copy(src, dst, self.locals.at[k])


class Remote:
    def __init__(self, copy, there, here):
        self.copy, self.there, self.here = copy, there, here
        self.waited = False

    def start(self):
        pl.when(self.there)(lambda: self.copy.start())

    def arrived(self):
        pl.when(self.here)(lambda: self.copy.wait_recv())

    def sent(self):
        self.waited = True
        pl.when(self.there)(lambda: self.copy.wait_send())


REMOTES = 22 + 2 * sum(map(len, FORWARD)) + 4 * sum(map(len, BACKWARD))
LOCALS = 5 + 2 * 3


def step_kernel(
    offs_ref, count_ref, step_ref, obj, probe_in, phase_in, amp_in, cos_in, sin_in, out,
    meta, near, probe, k, amp, cos, sin, fwd, bwd, src, mid, psi,
    hl, hr, body0, body1, xs, xr, ss, sr, placed, ends_raw, share,
    orr, ox, own_l, own_r, gl0, gl1, gr0, gr1, near_l, near_r,
    sends, receives, locals_,
):
    n = cos.shape[0]
    tile_rows, inner = obj.shape[2:]
    wide = inner + 2 * H
    tall = tile_rows + 2 * H
    half = (tall - n) // 2
    last = tile_rows - H
    bodies, gls, grs = (body0, body1), (gl0, gl1), (gr0, gr1)

    me_r, me_c = lax.axis_index("rows"), lax.axis_index("cols")
    n_r, n_c = lax.axis_size("rows"), lax.axis_size("cols")
    odd = lax.rem(me_r, 2)
    even = odd == 0
    side = 1 - 2 * odd
    has_left, has_right = me_c > 0, me_c < n_c - 1
    has_above, has_below = me_r > 0, me_r < n_r - 1
    far_above, far_below = me_r > 1, me_r < n_r - 2
    row = lambda r: {"rows": r, "cols": me_c}
    col = lambda c: {"rows": me_r, "cols": c}
    partner = row(me_r + side)
    outward = row(me_r - 2 * side)
    inward = row(me_r + 2 * side)
    has_outward = jnp.where(even, me_r - 2, n_r - 3 - me_r) >= 0
    has_inward = jnp.where(even, n_r - 3 - me_r, me_r - 2) >= 0
    always = me_r >= 0

    copies = Copies(sends, receives, locals_)
    far_rows = pl.ds(pl.multiple_of(odd * last, H), H)
    mate_rows = pl.ds(pl.multiple_of((1 - odd) * last, H), H)
    mid_rows = pl.ds(H, last - H)
    pieces = (far_rows, mate_rows, mid_rows)

    loads = [[copies.local(obj.at[s, :, at, :], out.at[s, :, at, :]) for at in pieces] for s in range(2)]
    load_small = [
        copies.local(a, b)
        for a, b in ((cos_in, cos), (sin_in, sin), (phase_in, k.at[0]), (probe_in, probe), (amp_in.at[0, 0, 0], amp))
    ]
    for c in loads[0][:2] + loads[1][:2] + load_small[:3] + loads[0][2:] + load_small[3:] + loads[1][2:]:
        c.start()
    for i in range(2):
        meta[i] = jnp.full(meta.shape[1:], offs_ref[i], jnp.int32)

    barrier = pltpu.get_barrier_semaphore()
    greeted = (
        (has_left, col(me_c - 1)), (has_right, col(me_c + 1)),
        (has_above, row(me_r - 1)), (has_below, row(me_r + 1)),
        (far_above, row(me_r - 2)), (far_below, row(me_r + 2)),
    )
    total = jnp.int32(0)
    for exists, device in greeted:
        total += exists.astype(jnp.int32)

        @pl.when(exists)
        def _(device=device):
            pl.semaphore_signal(barrier, inc=1, device_id=device, device_id_type=MESH)

    first_row = tall - n - H

    @pl.when(jnp.logical_not(has_left))
    def _():
        hl[...] = jnp.zeros_like(hl)
        near_l[...] = jnp.zeros_like(near_l)
        for ref in gls:
            ref[:, first_row : first_row + n, :] = jnp.zeros((2, n, H), F32)

    @pl.when(jnp.logical_not(has_right))
    def _():
        hr[...] = jnp.zeros_like(hr)
        near_r[...] = jnp.zeros_like(near_r)
        for ref in grs:
            ref[:, first_row : first_row + n, :] = jnp.zeros((2, n, H), F32)

    @pl.when(jnp.logical_not(has_inward))
    def _():
        xr[...] = jnp.zeros_like(xr)

    @pl.when(jnp.logical_not(has_outward))
    def _():
        ox[...] = jnp.zeros_like(ox)

    for i, exists in enumerate((has_above, has_below, has_left, has_right)):

        @pl.when(jnp.logical_not(exists))
        def _(i=i):
            near[i] = jnp.zeros(near.shape[1:], jnp.int32)

    pl.semaphore_wait(barrier, total)

    to_right = lambda a, b: copies.remote(a, b, has_right, has_left, col(me_c + 1))
    to_left = lambda a, b: copies.remote(a, b, has_left, has_right, col(me_c - 1))
    metas = [
        copies.remote(meta, near.at[0], has_below, has_above, row(me_r + 1)),
        copies.remote(meta, near.at[1], has_above, has_below, row(me_r - 1)),
        to_right(meta, near.at[2]),
        to_left(meta, near.at[3]),
    ]
    def halo(s, at, p=slice(None)):
        return [
            to_right(obj.at[s, p, at, inner - H :], hl.at[s, p, at, :]),
            to_left(obj.at[s, p, at, 0:H], hr.at[s, p, at, :]),
        ]

    halos = [[halo(s, at) for at in pieces] if s else [None] + [halo(s, at) for at in pieces[1:]] for s in range(2)]
    halo_first = [halo(0, far_rows, p) for p in range(2)]
    halos[0][0] = halo_first[0] + halo_first[1]
    for group in (metas, halos[0][0], halos[0][1], halos[1][0], halos[1][1], halos[0][2], halos[1][2]):
        for c in group:
            c.start()

    tiles = n // LANES + 1
    long = placed.shape[1]

    @pl.loop(0, 2 * tiles)
    def _(q):
        placed[q, :first_row, :] = jnp.zeros((first_row, LANES), F32)
        placed[q, first_row + n :, :] = jnp.zeros((first_row, LANES), F32)

    placed[2 * tiles] = jnp.zeros((long, LANES), F32)
    for lo, hi in ((0, first_row), (first_row + n, long)):
        for ref in gls + grs:
            ref[:, lo:hi, :] = jnp.zeros((2, hi - lo, H), F32)
    for lo in (0, 3 * H):
        ends_raw[:, :, lo : lo + H, :] = jnp.zeros((2, n // LANES, H, LANES), F32)

    my_row, my_col = offs_ref[0], offs_ref[1]
    weight = jnp.where(count_ref[0] > 0, 1.0, 0.0).astype(F32)
    for c in metas:
        c.arrived()
    above_row, above_col = jnp.max(near[0, 0]), jnp.max(near[0, 1])
    below_row, below_col = jnp.max(near[1, 0]), jnp.max(near[1, 1])
    left_row, right_row = jnp.max(near[2, 0]), jnp.max(near[3, 0])
    mate_row = jnp.where(even, below_row, above_row)
    mate_col = jnp.where(even, below_col, above_col)
    far_col = jnp.where(even, above_col, below_col)

    def take_columns(s, p, at, start):
        line = jnp.concatenate([hl[s, p, at, :], out[s, p, at, :], hr[s, p, at, :]], axis=1)
        return pltpu.roll(line, lax.rem(wide - start, wide), axis=1)[:, :n]

    def take_rows(field, part, start, height):
        strips = [field[part, q, pl.ds(start, height), :] for q in range(n // LANES)]
        return jnp.concatenate(strips, axis=1)

    def put_rows(field, part, rows, value):
        for q in range(n // LANES):
            field[part, q, rows, :] = value[:, q * LANES : (q + 1) * LANES]

    along = lambda chunks, source, target, there, here, device: [
        copies.remote(source.at[p, pl.ds(h, size)], target.at[p, pl.ds(h, size)], there, here, device)
        for p, h, size in chunks
    ]
    outers = [along(FORWARD[s], xs.at[s], xr.at[s], has_outward, has_inward, outward) for s in range(2)]
    inners = [along(FORWARD[s], ss.at[s], sr.at[s], always, always, partner) for s in range(2)]
    def send_far(s):
        loads[s][0].wait()
        if s:
            for c in halos[s][0]:
                c.arrived()
        for i, (p, h, size) in enumerate(FORWARD[s]):
            if not s and h == 0:
                for c in halo_first[p]:
                    c.arrived()
            at = pl.ds(pl.multiple_of(odd * last + h, SUBLANES), size)
            xs[s, p, pl.ds(h, size)] = take_columns(s, p, at, far_col)
            outers[s][i].start()

    def take_mate(s):
        loads[s][1].wait()
        for c in halos[s][1]:
            c.arrived()
        for p in range(2):
            ss[s, p] = take_columns(s, p, mate_rows, mate_col)

    send_far(0)
    take_mate(0)
    mate_near = jnp.where(even, mate_row <= half, mate_row > half)

    def pass_on(s, *which):
        for i in which:
            p, h, size = FORWARD[s][i]
            at = pl.ds(h, size)
            outers[s][i].arrived()
            ss[s, p, at] = jnp.where(mate_near, ss[s, p, at], xr[s, p, at])
            inners[s][i].start()

    def propagator(lo, hi):
        @pl.loop(lo // LANES, hi // LANES)
        def _(i):
            at = pl.ds(pl.multiple_of(i * LANES, LANES), LANES)
            phase = k[0, at, :]
            k[1, at, :] = jnp.sin(phase)
            k[0, at, :] = jnp.cos(phase)

    def fill_body(s, p):
        for lo in (0, last):
            put_rows(bodies[s], p, slice(H + lo, 2 * H + lo), take_columns(s, p, slice(lo, lo + H), my_col))

        @pl.loop(0, (last - H) // H)
        def _(i):
            at = pl.ds(pl.multiple_of(H + i * H, H), H)
            to = pl.ds(pl.multiple_of(2 * H + i * H, H), H)
            put_rows(bodies[s], p, to, take_columns(s, p, at, my_col))

    def body_ready(s):
        loads[s][2].wait()
        for c in halos[s][2]:
            c.arrived()

    pass_on(0, 0)
    send_far(1)
    pass_on(0, 1)
    take_mate(1)
    pass_on(0, 2)
    for c in load_small:
        c.wait()
    make_tables(cos, sin, fwd, bwd)
    propagator(0, n // 2)
    pass_on(0, 3)
    propagator(n // 2, n)
    pass_on(0, 4)
    body_ready(0)
    fill_body(0, 0)
    fill_body(0, 1)

    def halo_rows(s):
        for c in inners[s]:
            c.arrived()
        for p in range(2):
            block = sr[s, p]
            put_rows(bodies[s], p, slice(0, H), block)
            put_rows(bodies[s], p, slice(tall - H, tall), block)

    window = lambda s, p, lo, height: take_rows(bodies[s], p, my_row + lo, height)
    full = lambda lo, height: (pl.ds(lo, height), pl.ds(n + lo, height))

    def stage_one(left, between=()):
        for i in range(2):
            mid[:, i * n : (i + 1) * n] = jnp.dot(
                left[i * n : (i + 1) * n, :], src[...], preferred_element_type=F32
            ).astype(BF16)
            for f in between[i : i + 1]:
                f()

    interior = ((H, n - H), (n + H, 2 * n - H))
    exterior = ((0, H), (n - H, n + H), (2 * n - H, 2 * n))

    def product(left, i, spans):
        rows = slice(i * n, (i + 1) * n)
        return jnp.dot(
            jnp.concatenate([left[rows, a:b] for a, b in spans], axis=1),
            jnp.concatenate([src[a:b, :] for a, b in spans], axis=0),
            preferred_element_type=F32,
        )

    def stage_two(right, spans, epilogue):
        rows = [mid[lo : lo + height, :] for lo, height in spans]
        rows = rows[0] if len(rows) == 1 else jnp.concatenate(rows, axis=0)
        result = jnp.dot(rows, right[...], preferred_element_type=F32)
        at = 0
        for lo, height in spans:
            epilogue(lo, height, result[at : at + height, :n], result[at : at + height, n:])
            at += height

    whole = [(0, n)]
    ends = [(0, H), (n - H, H)]
    middle = [(H, n - 2 * H)]

    halo_rows(0)
    pass_on(1, 0)

    @pl.loop(0, n // H)
    def _(i):
        at = pl.ds(pl.multiple_of(i * H, H), H)
        low = pl.ds(pl.multiple_of(n + i * H, H), H)
        a_re = window(0, 0, i * H, H)
        a_im = window(0, 1, i * H, H)
        q_re, q_im = probe[0, at, :], probe[1, at, :]
        src[at, :] = (q_re * a_re - q_im * a_im).astype(BF16)
        src[low, :] = (q_re * a_im + q_im * a_re).astype(BF16)

    def propagate(lo, height, re, im):
        at, low = full(lo, height)
        k_re, k_im = k[0, at, :], k[1, at, :]
        src[at, :] = (re * k_re - im * k_im).astype(BF16)
        src[low, :] = (re * k_im + im * k_re).astype(BF16)

    def keep(lo, height, re, im):
        at, _ = full(lo, height)
        psi[0, at, :] = re
        psi[1, at, :] = im

    def exit_wave(lo, height):
        at, low = full(lo, height)
        b_re = window(1, 0, lo, height)
        b_im = window(1, 1, lo, height)
        p_re, p_im = psi[0, at, :], psi[1, at, :]
        src[at, :] = (p_re * b_re - p_im * b_im).astype(BF16)
        src[low, :] = (p_re * b_im + p_im * b_re).astype(BF16)

    stage_one(fwd)
    stage_two(bwd, whole, propagate)
    pass_on(1, 1)
    stage_one(bwd)
    body_ready(1)
    fill_body(1, 0)
    pass_on(1, 2)
    stage_two(fwd, whole, keep)
    pass_on(1, 3)
    fill_body(1, 1)
    for lo in range(H, n - H, H):
        exit_wave(lo, H)
    for i in range(2):
        share[i] = product(fwd, i, interior)
    halo_rows(1)
    for lo in (0, n - H):
        exit_wave(lo, H)

    def detect(lo, height, re, im):
        at, low = full(lo, height)
        factor = 1.0 - amp[at, :].astype(F32) / jnp.sqrt(re * re + im * im + 1.0)
        src[at, :] = (re * factor).astype(BF16)
        src[low, :] = (im * factor).astype(BF16)

    turn = lax.rem(my_col, LANES)

    def emit(s, p, lo, height, value):
        lane = lax.broadcasted_iota(jnp.int32, (height, LANES), 1)
        zero = jnp.zeros((height, LANES), F32)
        pieces = [value[:, q * LANES : (q + 1) * LANES] for q in range(n // LANES)]
        turned = [pltpu.roll(piece, turn, axis=1) for piece in pieces]
        at = pl.ds(first_row + lo, height)
        for q in range(tiles):
            before = turned[q - 1] if q else zero
            here = turned[q] if q < tiles - 1 else zero
            placed[p * tiles + q, at, :] = jnp.where(lane >= turn, here, before)
        own_l[s, p, pl.ds(lo, height), :] = jnp.where(lane >= my_col, turned[0], 0.0)
        own_r[s, p, pl.ds(lo, height), :] = jnp.where(lane < my_col - (inner + H - n), turned[-1], 0.0)
        if (lo, height) in ends:
            for q, piece in enumerate(pieces):
                ends_raw[p, q, pl.ds(H if lo == 0 else 2 * H, H), :] = piece

    def spread(lo, height, re, im):
        at, low = full(lo, height)
        p_re, p_im = psi[0, at, :], psi[1, at, :]
        b_re = window(1, 0, lo, height)
        b_im = window(1, 1, lo, height)
        emit(1, 0, lo, height, weight * (p_re * re + p_im * im))
        emit(1, 1, lo, height, weight * (p_re * im - p_im * re))
        src[at, :] = (b_re * re + b_im * im).astype(BF16)
        src[low, :] = (b_re * im - b_im * re).astype(BF16)

    spills = [along(BACKWARD[s], ss.at[s], orr.at[s], always, always, partner) for s in range(2)]
    relays = [along(BACKWARD[s], orr.at[s], ox.at[s], has_inward, has_outward, inward) for s in range(2)]
    early = [
        [
            to_left(own_l.at[s], grs[s].at[:, first_row : first_row + n, :]),
            to_right(own_r.at[s], gls[s].at[:, first_row : first_row + n, :]),
        ]
        for s in range(2)
    ]
    lates = [
        [
            [
                to_left(xs.at[s, p, pl.ds(h, size), : 2 * H], near_r.at[s, p, pl.ds(h, size)]),
                to_right(xs.at[s, p, pl.ds(h, size), 2 * H : 4 * H], near_l.at[s, p, pl.ds(h, size)]),
            ]
            for p, h, size in BACKWARD[s]
        ]
        for s in range(2)
    ]

    def spill(s):
        lower = tile_rows + 4 * H - n - jnp.maximum(my_row, tall - n - H)
        start = jnp.where(my_row <= half, H - jnp.minimum(my_row, H), lower)
        for c in inners[s]:
            c.sent()
        for i, (p, h, size) in enumerate(BACKWARD[s]):
            ss[s, p, pl.ds(h, size)] = take_rows(ends_raw, p, start + h, size)
            spills[s][i].start()

    def relay(s, *which):
        for i in which:
            spills[s][i].arrived()
            relays[s][i].start()

    def back(lo, height, re, im):
        at, low = full(lo, height)
        k_re, k_im = k[0, at, :], k[1, at, :]
        src[at, :] = (re * k_re + im * k_im).astype(BF16)
        src[low, :] = (im * k_re - re * k_im).astype(BF16)

    def finish(lo, height, re, im):
        at, _ = full(lo, height)
        q_re, q_im = probe[0, at, :], probe[1, at, :]
        emit(0, 0, lo, height, weight * (q_re * re + q_im * im))
        emit(0, 1, lo, height, weight * (q_re * im - q_im * re))

    spread_out = lambda block, start: pltpu.roll(
        jnp.concatenate([block, jnp.zeros((block.shape[0], wide - n), F32)], axis=1), start, axis=1
    )

    column = sum(jnp.where(my_col >= q * LANES, 1, 0) for q in range(1, (wide - n) // LANES + 1))

    def place_own(s, p):
        @pl.loop(0, tile_rows // H)
        def _(i):
            at = pl.ds(pl.multiple_of(i * H, H), H)
            for j in range(inner // LANES):
                tile = j + H // LANES - column
                inside = jnp.logical_and(tile >= 0, tile < tiles)
                tile = jnp.where(inside, p * tiles + tile, 2 * tiles)
                block = placed[tile, pl.ds(tall - n - my_row + i * H, H), :]
                lanes = slice(j * LANES, (j + 1) * LANES)
                out[s, p, at, lanes] -= step_ref[s] * block

    def place_near(s, i):
        p, h, size = BACKWARD[s][i]
        at = pl.ds(h, size)
        relays[s][i].arrived()
        for e, mine, start in (
            (0, jnp.logical_and(has_above, above_row > half), above_col),
            (1, jnp.logical_and(has_below, below_row <= half), below_col),
        ):
            outer = even if e == 0 else jnp.logical_not(even)
            block = jnp.where(outer, ox[s, p, at], orr[s, p, at])
            block = spread_out(jnp.where(mine, block, jnp.zeros_like(block)), start)
            xs[s, p, at, e * H : (e + 1) * H] = block[:, :H]
            xs[s, p, at, (2 + e) * H : (3 + e) * H] = block[:, H + inner :]
            rows = pl.ds(e * last + h, size)
            out[s, p, rows, :] -= step_ref[s] * block[:, H : H + inner]
        for c in lates[s][i]:
            c.start()

    def sides(s):
        for c in early[s]:
            c.arrived()
        for p in range(2):

            @pl.loop(0, tile_rows // H)
            def _(i, p=p):
                at = pl.ds(pl.multiple_of(i * H, H), H)
                from_left = gls[s][p, pl.ds(tall - n - left_row + i * H, H), :]
                from_right = grs[s][p, pl.ds(tall - n - right_row + i * H, H), :]
                out[s, p, at, :H] -= step_ref[s] * from_left
                out[s, p, at, inner - H :] -= step_ref[s] * from_right

    def corners(s, i):
        p, h, size = BACKWARD[s][i]
        for c in lates[s][i]:
            c.arrived()
        for e in range(2):
            at = pl.ds(e * last + h, size)
            out[s, p, at, :H] -= step_ref[s] * near_l[s, p, pl.ds(h, size), e * H : (e + 1) * H]
            out[s, p, at, inner - H :] -= step_ref[s] * near_r[s, p, pl.ds(h, size), e * H : (e + 1) * H]

    for i in range(2):
        mid[:, i * n : (i + 1) * n] = (share[i] + product(fwd, i, exterior)).astype(BF16)
    stage_two(bwd, whole, detect)
    stage_one(bwd)
    stage_two(fwd, ends, spread)
    spill(1)
    stage_two(fwd, middle, spread)
    for c in early[1]:
        c.start()
    stage_one(fwd)
    relay(1, 0)
    stage_two(bwd, whole, back)
    place_own(1, 0)
    relay(1, 1)
    place_own(1, 1)
    stage_one(bwd)
    stage_two(fwd, ends, finish)
    spill(0)
    relay(1, 2)
    stage_two(fwd, middle, finish)
    for c in early[0]:
        c.start()
    for c in outers[0] + outers[1]:
        c.sent()
    relay(1, 3)
    place_near(1, 0)
    place_near(1, 1)
    place_own(0, 0)
    relay(0, 0)
    place_near(1, 2)
    place_near(1, 3)
    place_own(0, 1)
    relay(0, 1)
    sides(1)
    relay(0, 2)
    place_near(0, 0)
    relay(0, 3)
    place_near(0, 1)
    relay(0, 4)
    place_near(0, 2)
    for i in range(4):
        corners(1, i)
    sides(0)
    for i in range(3, 5):
        place_near(0, i)
    for i in range(5):
        corners(0, i)

    for c in copies.remotes:
        if not c.waited:
            c.sent()
    assert len(copies.remotes) == REMOTES and copies.local_used == LOCALS


def write_kernel(done, out, sems):
    copies = []
    rows = done.shape[2] // 3
    for i in range(12):
        at = (i // 6, i // 3 % 2, pl.ds(i % 3 * rows, rows))
        copies.append(pltpu.make_async_copy(done.at[at], out.at[at], sems.at[i]))
    for c in copies:
        c.start()
    for c in copies:
        c.wait()


def per_device(object_tiles, probe, prop_phase, amplitudes, offsets, counts, step_size):
    n = probe.shape[1]
    rows, inner = object_tiles.shape[2:]
    cos, sin = dft_table(n)
    tall = rows + 2 * H
    smem = pl.BlockSpec(memory_space=pltpu.SMEM)
    anywhere = pl.BlockSpec(memory_space=pl.ANY)
    on_chip = pl.BlockSpec(memory_space=pltpu.VMEM)
    vmem = lambda *shape, kind=F32: pltpu.VMEM(shape, kind)
    block = vmem(2, 2, H, n)
    long = 2 * tall - n - 2 * H
    scratch = (
        [vmem(2, SUBLANES, LANES, kind=jnp.int32), vmem(4, 2, SUBLANES, LANES, kind=jnp.int32)]
        + [vmem(2, n, n), vmem(2, n, n)]
        + [vmem(n, n, kind=BF16)] * 3
        + [vmem(2 * n, 2 * n, kind=BF16)] * 2
        + [vmem(2 * n, n, kind=BF16), vmem(n, 2 * n, kind=BF16), vmem(2, n, n)]
        + [vmem(2, 2, rows, H)] * 2
        + [vmem(2, n // LANES, tall, LANES)] * 2
        + [block] * 4
        + [vmem(2 * (n // LANES + 1) + 1, long, LANES), vmem(2, n // LANES, 4 * H, LANES), vmem(2, n, n)]
        + [block] * 2
        + [vmem(2, 2, n, H)] * 2
        + [vmem(2, long, H)] * 4
        + [vmem(2, 2, H, 2 * H)] * 2
        + [pltpu.SemaphoreType.DMA((REMOTES,))] * 2
        + [pltpu.SemaphoreType.DMA((LOCALS,))]
    )
    done = pl.pallas_call(
        step_kernel,
        in_specs=[smem] * 3 + [anywhere] * 6,
        out_specs=on_chip,
        out_shape=pltpu.VMEM(object_tiles.shape, F32),
        scratch_shapes=scratch,
        name="step",
        compiler_params=pltpu.CompilerParams(
            collective_id=0, has_side_effects=True, vmem_limit_bytes=VMEM_LIMIT
        ),
    )(offsets[0, 0, 0], counts[0], step_size, object_tiles, probe, prop_phase, amplitudes, cos, sin)
    return pl.pallas_call(
        write_kernel,
        in_specs=[on_chip],
        out_specs=anywhere,
        out_shape=jax.ShapeDtypeStruct(object_tiles.shape, F32),
        scratch_shapes=[pltpu.SemaphoreType.DMA((12,))],
        name="write",
        compiler_params=pltpu.CompilerParams(vmem_limit_bytes=1 << 20),
    )(done)


VMEM_LIMIT = 54 << 20


def solution(mesh):
    return jax.shard_map(
        per_device,
        mesh=mesh,
        in_specs=(
            P(None, None, "rows", "cols"),
            P(),
            P(),
            P("rows", "cols", None, None, None),
            P("rows", "cols", None, None),
            P("rows", "cols"),
            P(),
        ),
        out_specs=P(None, None, "rows", "cols"),
        check_vma=False,
    )
```
